1024 devices in a mesh: slab: 128 (over x, z), chan: 8 (over y, core).
Axes of the slice: x: 4, y: 4, z: 32, core: 2. Of those that a mesh axis runs over, the one named last changes fastest.
Arguments:
- volume: bfloat16 [64, 128, 16, 128], P('chan', 'slab'), may hold values from -6 to 6
- kernel: bfloat16 [3, 3, 3, 64, 128], P(None, None, None, None, 'chan'), may hold values from -0.15625 to 0.15625
- bias: float32 [128], P('chan'), may hold values from -3 to 3
- out_grad: bfloat16 [128, 128, 16, 128], P('chan', 'slab'), may hold values from -6 to 6
Outputs:
- feature: bfloat16 [128, 128, 16, 128], P('chan', 'slab')
- input_grad: bfloat16 [64, 128, 16, 128], P('chan', 'slab')
- kernel_grad: float32 [3, 3, 3, 64, 128], P(None, None, None, None, 'chan')
- bias_grad: float32 [128], P('chan')
The draws below stay inside these ranges and needn't reach their ends.
All inputs are finite; a program needn't handle non-finite values.
Results may differ from the reference program's by a relative error of at most 0.00105.
Values may be sent and summed in bfloat16 or wider, within the bound.
No kernel may reach another device: no remote copies, remote signals or barrier semaphores. Data moves between devices by JAX's collectives and lax.ppermute only.
A program may use at most 32 MiB of HBM per device.

```python
import jax
import jax.numpy as jnp
from jax import lax

CIN = 64
COUT = 128
ROWS = 16
COLS = 128
DEPTH = 128


def steps_of(key, extent, cuts, low, top_value):
    def one(position, blocks):
        steps = jax.random.uniform(jax.random.fold_in(jax.random.fold_in(key, 6), position), (blocks,), jnp.float32, low / len(cuts), top_value / len(cuts))
        return jnp.repeat(jnp.exp(steps), extent[position] // blocks).reshape((-1,) + (1,) * (len(extent) - position - 1))

    level = one(*cuts[0])
    for cut in cuts[1:]:
        level = level * one(*cut)
    return level


def bell_draw(rng, shape, scale, reach, pieces=(), held_as=jnp.bfloat16):
    result = jax.random.normal(rng, shape, jnp.float32) * scale
    if len(pieces) > 0:
        result = steps_of(rng, shape, pieces, -0.22, 0.18) * result
    return jnp.clip(result, min=-reach, max=reach).astype(held_as)


def setup_inputs(seed: int = 0) -> dict:
    key_list = jax.random.split(jax.random.key(seed), 5)
    volume = bell_draw(key_list[0], (CIN, DEPTH, ROWS, COLS), 1.0, 6.0, ((0, 8), (1, 128)))
    kernel = bell_draw(key_list[1], (3, 3, 3, CIN, COUT), (27 * CIN) ** -0.5, 0.15625, ((4, 8),))
    bias = bell_draw(key_list[2], (COUT,), 0.5, 3.0, ((0, 8),), jnp.float32)
    out_grad = bell_draw(key_list[3], (COUT, DEPTH, ROWS, COLS), 1.0, 6.0, ((0, 8), (1, 128)))
    return {"volume": volume, "kernel": kernel, "bias": bias, "out_grad": out_grad}


def convolve(volume_f, kernel_f):
    return lax.conv_general_dilated(volume_f[None], kernel_f, (1, 1, 1), ((1, 1), (1, 1), (1, 1)), dimension_numbers=('NCDHW', 'DHWIO', 'NCDHW'), precision=lax.Precision.HIGHEST)[0]

def reference(volume, kernel, bias, out_grad):
    volume_f = volume.astype(jnp.float32)
    kernel_f = kernel.astype(jnp.float32)
    pre, pullback = jax.vjp(convolve, volume_f, kernel_f)
    feature = (pre + bias[:, None, None, None]).astype(jnp.bfloat16)
    grad_f = out_grad.astype(jnp.float32)
    volume_grad, weight_grad = pullback(grad_f)
    factor = 1.0 / jnp.sqrt(jnp.float32(DEPTH * ROWS * COLS))
    bias_grad = lax.optimization_barrier(jnp.sum(grad_f, axis=(1, 2, 3))) * factor
    return (feature, volume_grad.astype(jnp.bfloat16), weight_grad * factor, bias_grad)
```

```python
import functools
import math

import jax
import jax.numpy as jnp
from jax import lax
from jax.experimental import pallas as pl
from jax.experimental.pallas import tpu as pltpu
from jax.sharding import Mesh, PartitionSpec as P

X, Z = 4, 32
ZL = 4
ZH = Z // ZL
SLAB = ("x", "zh", "zl")
NEAR = ("x", "zl")
ROWS, COLS = 16, 128
CELLS = ROWS * COLS
F32, BF16 = jnp.float32, jnp.bfloat16


def call(body, outs, args, scratch=(), flops=0):
    moved = sum(math.prod(a.shape) * a.dtype.itemsize for a in (*args, *outs))
    return pl.pallas_call(
        body,
        out_shape=tuple(outs),
        in_specs=[pl.BlockSpec(memory_space=pltpu.VMEM)] * len(args),
        out_specs=tuple(pl.BlockSpec(memory_space=pltpu.VMEM) for _ in outs),
        scratch_shapes=list(scratch),
        compiler_params=pltpu.CompilerParams(vmem_limit_bytes=24 << 20),
        cost_estimate=pl.CostEstimate(flops=flops, bytes_accessed=moved, transcendentals=0),
    )(*args)


def shape(dims, dtype):
    return jax.ShapeDtypeStruct(dims, dtype)


def cells_to_lanes(value, spare):
    count = value.shape[0]
    spare[...] = value.astype(F32).reshape(count * ROWS, COLS)
    rows = [spare[pl.ds(h, count, stride=ROWS), :] for h in range(ROWS)]
    return jnp.concatenate(rows, axis=1).astype(BF16)


def lanes_to_cells(value, spare):
    count = value.shape[0]
    for h in range(ROWS):
        spare[pl.ds(h, count, stride=ROWS), :] = value[:, h * COLS : (h + 1) * COLS]
    return spare[...].reshape(count, 1, ROWS, COLS).astype(BF16)


def from_row(value, step):
    if step == 0:
        return value
    gap = jnp.zeros((value.shape[0], COLS), value.dtype)
    if step > 0:
        return jnp.concatenate([value[:, COLS:], gap], axis=1)
    return jnp.concatenate([gap, value[:, :-COLS]], axis=1)


def from_col(value, step):
    if step == 0:
        return value
    lane = lax.broadcasted_iota(jnp.int32, (value.shape[0], COLS), 1)
    keep = lane != (COLS - 1 if step > 0 else 0)
    parts = []
    for h in range(ROWS):
        part = value[:, h * COLS : (h + 1) * COLS].astype(F32)
        part = pltpu.roll(part, (-step) % COLS, axis=1)
        parts.append(jnp.where(keep, part, 0.0).astype(value.dtype))
    return jnp.concatenate(parts, axis=1)


def pack_body(volume, grad, volume_out, grad_out, spare_v, spare_g):
    flat = cells_to_lanes(volume[...], spare_v)
    for k in range(volume_out.shape[0]):
        volume_out[k] = flat
    grad_out[...] = cells_to_lanes(grad[...], spare_g)


def kernel_grad_body(volume, after, here, before, out):
    left = jnp.concatenate(
        [from_row(g[...], 1 - b) for g in (after, here, before) for b in range(3)], axis=0
    )
    right = jnp.concatenate([from_col(volume[...], c - 1) for c in range(3)], axis=0)
    sums = lax.dot_general(left, right, (((1,), (1,)), ((), ())), preferred_element_type=F32)
    out[0:144] = sums[:, 0:128]
    out[144:216] = jnp.concatenate([sums[0:72, 128:192], sums[72:144, 128:192]], axis=1)
    total = jnp.sum(here[...].astype(F32), axis=1, keepdims=True)
    wide = jnp.broadcast_to(total, (16, 128))
    row = lax.broadcasted_iota(jnp.int32, (16, 128), 0)
    lane = lax.broadcasted_iota(jnp.int32, (16, 128), 1)
    across = jnp.sum(jnp.where(row == lane, wide, 0.0), axis=0, keepdims=True)
    out[216:224] = jnp.broadcast_to(across, (8, 128))
    out[224:] = jnp.zeros((out.shape[0] - 224, 128), F32)


def sum_body(factor, parts, out):
    total = parts[0]
    for k in range(1, parts.shape[0]):
        total = total + parts[k]
    if factor is not None:
        total = total * factor
    for k in range(out.shape[0]):
        out[k] = total


def unpack_body(flat, kernel_out, bias_out):
    for a in range(3):
        for b in range(3):
            for half in range(2):
                r = (a * 3 + b) * 16 + half * 8
                o = slice(half * 8, half * 8 + 8)
                pair = flat[r : r + 8]
                kernel_out[a, b, 0, o] = pair[:, 0:64]
                kernel_out[a, b, 1, o] = pair[:, 64:128]
                if r < 72:
                    kernel_out[a, b, 2, o] = flat[144 + r : 152 + r][:, 0:64]
                else:
                    kernel_out[a, b, 2, o] = flat[72 + r : 80 + r][:, 64:128]
    bias_out[...] = flat[216:217]


def input_grad_body(kernel, after, here, before, out):
    left = jnp.concatenate([kernel[:, b].reshape(144, 64) for b in range(3)], axis=1)
    right = jnp.concatenate(
        [from_col(g[...], 1 - c) for g in (after, here, before) for c in range(3)], axis=0
    )
    sums = lax.dot_general(left, right, (((0,), (0,)), ((), ())), preferred_element_type=F32)
    total = sums[64:128]
    total = total + from_row(sums[0:64], 1)
    out[...] = total + from_row(sums[128:192], -1)


def feature_body(kernel, bias, before, here, after, out, spare):
    left = jnp.concatenate([kernel[a].reshape(144, 64) for a in range(3)], axis=1)
    right = jnp.concatenate([before[...], here[...], after[...]], axis=0)
    sums = jnp.dot(left, right, preferred_element_type=F32)
    total = None
    for c in (1, 0, 2):
        part = None
        for b in range(3):
            r = (b * 3 + c) * 16
            term = from_row(sums[r : r + 16], b - 1)
            part = term if part is None else part + term
        part = from_col(part, c - 1)
        total = part if total is None else total + part
    row = lax.broadcasted_iota(jnp.int32, (16, 128), 0)
    lane = lax.broadcasted_iota(jnp.int32, (16, 128), 1)
    column = jnp.sum(jnp.where(row == lane, bias[...], 0.0), axis=1, keepdims=True)
    out[...] = lanes_to_cells(total + column, spare)


def narrow_body(value, out, spare):
    out[...] = lanes_to_cells(value[...], spare)


def on_device(volume, kernel, bias, out_grad):
    slabs = X * Z
    groups = lax.axis_size("chan")
    up = [(i, i + 1) for i in range(slabs - 1)]
    down = [(i + 1, i) for i in range(slabs - 1)]
    weights = jnp.transpose(kernel, (0, 1, 2, 4, 3))

    sent, here = call(
        pack_body,
        [shape((groups, 8, CELLS), BF16), shape((16, CELLS), BF16)],
        [volume, out_grad],
        [pltpu.VMEM((8 * ROWS, COLS), F32), pltpu.VMEM((16 * ROWS, COLS), F32)],
    )
    before = lax.ppermute(here, SLAB, up)
    after = lax.ppermute(here, SLAB, down)
    whole = lax.all_to_all(sent, "chan", 0, 0).reshape(64, CELLS)

    (partial,) = call(
        kernel_grad_body,
        [shape((256, 128), F32)],
        [whole, after, here, before],
        flops=2 * 144 * 192 * CELLS,
    )
    near = X * ZL
    rows = 256 // near
    parts = lax.all_to_all(partial.reshape(near, rows, 128), NEAR, 0, 0)
    (spread,) = call(
        functools.partial(sum_body, None), [shape((ZH, rows, 128), F32)], [parts]
    )
    parts = lax.all_to_all(spread, "zh", 0, 0)
    factor = 1.0 / math.sqrt(slabs * CELLS)
    (spread,) = call(
        functools.partial(sum_body, factor), [shape((near, rows, 128), F32)], [parts]
    )
    flat = lax.all_to_all(spread, NEAR, 0, 0).reshape(256, 128)
    kernel_out, bias_out = call(
        unpack_body, [shape((3, 3, 3, 16, 64), F32), shape((1, 128), F32)], [flat]
    )

    (share,) = call(
        input_grad_body,
        [shape((64, CELLS), F32)],
        [weights, after, here, before],
        flops=2 * 144 * 192 * CELLS,
    )
    mine = lax.psum_scatter(share, "chan", scatter_dimension=0, tiled=True)
    (input_grad,) = call(
        narrow_body,
        [shape((8, 1, ROWS, COLS), BF16)],
        [mine],
        [pltpu.VMEM((8 * ROWS, COLS), F32)],
    )

    whole_before = lax.ppermute(whole, SLAB, up)
    whole_after = lax.ppermute(whole, SLAB, down)
    (feature,) = call(
        feature_body,
        [shape((16, 1, ROWS, COLS), BF16)],
        [weights, jnp.pad(bias, (0, 112)).reshape(1, 128), whole_before, whole, whole_after],
        [pltpu.VMEM((16 * ROWS, COLS), F32)],
        flops=2 * 144 * 192 * CELLS,
    )
    return (
        feature,
        input_grad,
        jnp.transpose(kernel_out, (0, 1, 2, 4, 3)),
        bias_out[0, :16],
    )


def solution(mesh):
    split = Mesh(mesh.devices.reshape(X, ZH, ZL, -1), ("x", "zh", "zl", "chan"))
    in_specs = (
        P("chan", SLAB, None, None),
        P(None, None, None, None, "chan"),
        P("chan"),
        P("chan", SLAB, None, None),
    )
    out_specs = (
        P("chan", SLAB, None, None),
        P("chan", SLAB, None, None),
        P(None, None, None, None, "chan"),
        P("chan"),
    )
    return jax.shard_map(
        on_device, mesh=split, in_specs=in_specs, out_specs=out_specs, check_vma=False
    )
```

```python
import functools
import math

import jax
import jax.numpy as jnp
from jax import lax
from jax.experimental import pallas as pl
from jax.experimental.pallas import tpu as pltpu
from jax.sharding import Mesh, PartitionSpec as P

X, Z = 4, 32
ZL = 4
ZH = Z // ZL
SLAB = ("x", "zh", "zl")
NEAR = ("x", "zl")
ROWS, COLS = 16, 128
CELLS = ROWS * COLS
F32, BF16 = jnp.float32, jnp.bfloat16


def call(body, outs, args, scratch=(), flops=0, after=(), anywhere=False, limit=24):
    used, late = (len(args), len(after))
    inner = body
    if late:
        def inner(*refs):
            body(*refs[:used], *refs[used + late :])
    args = [*args, *after]
    space = pltpu.HBM if anywhere else pltpu.VMEM
    moved = sum(math.prod(a.shape) * a.dtype.itemsize for a in (*args, *outs))
    return pl.pallas_call(
        inner,
        out_shape=tuple(outs),
        in_specs=[pl.BlockSpec(memory_space=space)] * used
        + [pl.BlockSpec(memory_space=pl.ANY)] * late,
        out_specs=tuple(pl.BlockSpec(memory_space=pltpu.VMEM) for _ in outs),
        scratch_shapes=list(scratch),
        compiler_params=pltpu.CompilerParams(vmem_limit_bytes=limit << 20),
        cost_estimate=pl.CostEstimate(flops=flops, bytes_accessed=moved, transcendentals=0),
    )(*args)


def shape(dims, dtype):
    return jax.ShapeDtypeStruct(dims, dtype)


def cells_to_lanes(value, spare):
    count = value.shape[0]
    spare[...] = value[...].astype(F32).reshape(count * ROWS, COLS)
    rows = [spare[pl.ds(h, count, stride=ROWS), :] for h in range(ROWS)]
    return jnp.concatenate(rows, axis=1).astype(BF16)


def lanes_to_cells(value, spare):
    count = value.shape[0]
    for h in range(ROWS):
        spare[pl.ds(h, count, stride=ROWS), :] = value[:, h * COLS : (h + 1) * COLS]
    return spare[...].reshape(count, 1, ROWS, COLS).astype(BF16)


def from_row(value, step):
    if step == 0:
        return value
    gap = jnp.zeros((value.shape[0], COLS), value.dtype)
    if step > 0:
        return jnp.concatenate([value[:, COLS:], gap], axis=1)
    return jnp.concatenate([gap, value[:, :-COLS]], axis=1)


def from_col(value, step):
    if step == 0:
        return value
    lane = lax.broadcasted_iota(jnp.int32, (value.shape[0], COLS), 1)
    keep = lane != (COLS - 1 if step > 0 else 0)
    parts = []
    for h in range(ROWS):
        part = value[:, h * COLS : (h + 1) * COLS].astype(F32)
        part = pltpu.roll(part, (-step) % COLS, axis=1)
        parts.append(jnp.where(keep, part, 0.0).astype(value.dtype))
    return jnp.concatenate(parts, axis=1)


def pack_body(volume, grad, volume_out, plane_out, here_v, here_g, spare_v, spare_g, sems):
    copy_g = pltpu.make_async_copy(grad, here_g, sems.at[0])
    copy_v = pltpu.make_async_copy(volume, here_v, sems.at[1])
    copy_v.start()
    copy_g.start()
    copy_v.wait()
    flat = cells_to_lanes(here_v, spare_v)
    for k in range(volume_out.shape[0]):
        volume_out[k] = flat
    plane_out[16:24] = flat
    copy_g.wait()
    plane_out[0:16] = cells_to_lanes(here_g, spare_g)


def kernel_grad_body(volume, after, here, before, out):
    left = jnp.concatenate(
        [from_row(g[0:16], 1 - b) for g in (after, here, before) for b in range(3)], axis=0
    )
    right = jnp.concatenate([from_col(volume[...], c - 1) for c in range(3)], axis=0)
    sums = lax.dot_general(left, right, (((1,), (1,)), ((), ())), preferred_element_type=F32)
    out[0:144] = sums[:, 0:128]
    out[144:216] = jnp.concatenate([sums[0:72, 128:192], sums[72:144, 128:192]], axis=1)
    total = jnp.sum(here[0:16].astype(F32), axis=1, keepdims=True)
    wide = jnp.broadcast_to(total, (16, 128))
    row = lax.broadcasted_iota(jnp.int32, (16, 128), 0)
    lane = lax.broadcasted_iota(jnp.int32, (16, 128), 1)
    across = jnp.sum(jnp.where(row == lane, wide, 0.0), axis=0, keepdims=True)
    out[216:224] = jnp.broadcast_to(across, (8, 128))
    out[224:] = jnp.zeros((out.shape[0] - 224, 128), F32)


def sum_body(factor, parts, out):
    total = parts[0]
    for k in range(1, parts.shape[0]):
        total = total + parts[k]
    if factor is not None:
        total = total * factor
    for k in range(out.shape[0]):
        out[k] = total


def unpack_body(flat, kernel_out, bias_out):
    for a in range(3):
        for b in range(3):
            for half in range(2):
                r = (a * 3 + b) * 16 + half * 8
                o = slice(half * 8, half * 8 + 8)
                pair = flat[r : r + 8]
                kernel_out[a, b, 0, o] = pair[:, 0:64]
                kernel_out[a, b, 1, o] = pair[:, 64:128]
                if r < 72:
                    kernel_out[a, b, 2, o] = flat[144 + r : 152 + r][:, 0:64]
                else:
                    kernel_out[a, b, 2, o] = flat[72 + r : 80 + r][:, 64:128]
    bias_out[...] = flat[216:217, 0:16]


def input_grad_body(kernel, after, here, before, kept, sent):
    left = jnp.concatenate([kernel[:, b].reshape(144, 64) for b in range(3)], axis=1)
    right = jnp.concatenate(
        [from_col(g[0:16], 1 - c) for g in (after, here, before) for c in range(3)], axis=0
    )
    sums = lax.dot_general(left, right, (((0,), (0,)), ((), ())), preferred_element_type=F32)
    total = sums[64:128]
    total = total + from_row(sums[0:64], 1)
    total = total + from_row(sums[128:192], -1)
    odd = lax.rem(lax.axis_index("chan"), 2) == 1
    for y in range(4):
        first, second = total[16 * y : 16 * y + 8], total[16 * y + 8 : 16 * y + 16]
        kept[y] = jnp.where(odd, second, first)
        sent[y], sent[4 + y] = halves(jnp.where(odd, first, second))
    sent[8] = before[16:24]
    sent[9] = after[16:24]


def halves(value):
    high = value.astype(BF16)
    return high, (value - high.astype(F32)).astype(BF16)


def join_body(kept, got, before, after, own, *sent):
    chan = lax.axis_index("chan")
    y, odd = lax.div(chan, 2), lax.rem(chan, 2) == 1
    for k, out in enumerate((own, *sent)):
        block = lax.rem(y + k, 4)
        total = kept[block] + got[block].astype(F32) + got[4 + block].astype(F32)
        if k == 0:
            out[...] = total
        else:
            out[0:8], out[8:16] = halves(total)
    for row, mine, theirs in ((16, before, got[8]), (32, after, got[9])):
        mine, theirs = mine[16:24].astype(F32), theirs.astype(F32)
        first = jnp.where(odd, theirs, mine).astype(BF16)
        second = jnp.where(odd, mine, theirs).astype(BF16)
        for out in sent:
            out[row : row + 8] = first
            out[row + 8 : row + 16] = second


def feature_body(kernel, bias, here, own, first, second, third, out, before, after, spare):
    y = lax.div(lax.axis_index("chan"), 2)
    for k, part in enumerate((own, first, second, third)):
        place = pl.ds(pl.multiple_of(16 * lax.rem(y + 4 - k, 4), 16), 16)
        before[place] = part[16:32]
        after[place] = part[32:48]
    left = jnp.concatenate([kernel[a].reshape(144, 64) for a in range(3)], axis=1)
    right = jnp.concatenate([before[...], here[...], after[...]], axis=0)
    sums = jnp.dot(left, right, preferred_element_type=F32)
    total = None
    for c in (1, 0, 2):
        part = None
        for b in range(3):
            r = (b * 3 + c) * 16
            term = from_row(sums[r : r + 16], b - 1)
            part = term if part is None else part + term
        part = from_col(part, c - 1)
        total = part if total is None else total + part
    row = lax.broadcasted_iota(jnp.int32, (16, 16), 0)
    lane = lax.broadcasted_iota(jnp.int32, (16, 16), 1)
    column = jnp.sum(jnp.where(row == lane, bias[...], 0.0), axis=1, keepdims=True)
    out[...] = lanes_to_cells(total + column, spare)


def narrow_body(own, first, second, third, out, spare):
    total = own[...]
    for part in (first, second, third):
        total = total + (part[0:8].astype(F32) + part[8:16].astype(F32))
    out[...] = lanes_to_cells(total, spare)


def on_device(volume, kernel, bias, out_grad):
    slabs = X * Z
    groups = lax.axis_size("chan")
    up = [(i, i + 1) for i in range(slabs - 1)]
    down = [(i + 1, i) for i in range(slabs - 1)]
    weights = jnp.transpose(kernel, (0, 1, 2, 4, 3))

    sent, here = call(
        pack_body,
        [shape((groups, 8, CELLS), BF16), shape((24, CELLS), BF16)],
        [volume, out_grad],
        [
            pltpu.VMEM(volume.shape, BF16),
            pltpu.VMEM(out_grad.shape, BF16),
            pltpu.VMEM((8 * ROWS, COLS), F32),
            pltpu.VMEM((16 * ROWS, COLS), F32),
            pltpu.SemaphoreType.DMA((2,)),
        ],
        anywhere=True,
        limit=60,
    )
    before = lax.ppermute(here, SLAB, up)
    after = lax.ppermute(here, SLAB, down)
    whole = lax.all_to_all(sent, "chan", 0, 0).reshape(64, CELLS)

    (partial,) = call(
        kernel_grad_body,
        [shape((256, 128), F32)],
        [whole, after, here, before],
        flops=2 * 144 * 192 * CELLS,
    )
    kept, sent = call(
        input_grad_body,
        [shape((4, 8, CELLS), F32), shape((10, 8, CELLS), BF16)],
        [weights, after, here, before],
        flops=2 * 144 * 192 * CELLS,
    )
    got = lax.ppermute(sent, "chan", [(i, i ^ 1) for i in range(groups)])
    near = X * ZL
    rows = 256 // near
    parts = lax.all_to_all(partial.reshape(near, rows, 128), NEAR, 0, 0)
    (spread,) = call(
        functools.partial(sum_body, None),
        [shape((ZH, rows, 128), F32)],
        [parts],
        after=[got],
    )
    parts = lax.all_to_all(spread, "zh", 0, 0)
    own, *joined = call(
        join_body,
        [shape((8, CELLS), F32)] + [shape((48, CELLS), BF16)] * 3,
        [kept, got, before, after],
        after=[spread],
    )
    others = [
        lax.ppermute(part, "chan", [(i, (i + 2 * k + 2) % groups) for i in range(groups)])
        for k, part in enumerate(joined)
    ]
    factor = 1.0 / math.sqrt(slabs * CELLS)
    (spread,) = call(
        functools.partial(sum_body, factor),
        [shape((near, rows, 128), F32)],
        [parts],
        after=[*others],
    )
    flat = lax.all_to_all(spread, NEAR, 0, 0).reshape(256, 128)
    kernel_out, bias_out = call(
        unpack_body, [shape((3, 3, 3, 16, 64), F32), shape((1, 16), F32)], [flat]
    )

    (input_grad,) = call(
        narrow_body,
        [shape((8, 1, ROWS, COLS), BF16)],
        [own, *others],
        [pltpu.VMEM((8 * ROWS, COLS), F32)],
    )

    (feature,) = call(
        feature_body,
        [shape((16, 1, ROWS, COLS), BF16)],
        [weights, bias.reshape(1, 16), whole, joined[0], *others],
        [
            pltpu.VMEM((64, CELLS), BF16),
            pltpu.VMEM((64, CELLS), BF16),
            pltpu.VMEM((16 * ROWS, COLS), F32),
        ],
        flops=2 * 144 * 192 * CELLS,
    )
    return (
        feature,
        input_grad,
        jnp.transpose(kernel_out, (0, 1, 2, 4, 3)),
        bias_out.reshape(16),
    )


def solution(mesh):
    split = Mesh(mesh.devices.reshape(X, ZH, ZL, -1), ("x", "zh", "zl", "chan"))
    in_specs = (
        P("chan", SLAB, None, None),
        P(None, None, None, None, "chan"),
        P("chan"),
        P("chan", SLAB, None, None),
    )
    out_specs = (
        P("chan", SLAB, None, None),
        P("chan", SLAB, None, None),
        P(None, None, None, None, "chan"),
        P("chan"),
    )
    return jax.shard_map(
        on_device, mesh=split, in_specs=in_specs, out_specs=out_specs, check_vma=False
    )
```

```python
import functools
import math

import jax
import jax.numpy as jnp
from jax import lax
from jax.experimental import pallas as pl
from jax.experimental.pallas import tpu as pltpu
from jax.sharding import Mesh, PartitionSpec as P

X, Z = 4, 32
ZL = 4
ZH = Z // ZL
SLAB = ("x", "zh", "zl")
NEAR = ("x", "zl")
ROWS, COLS = 16, 128
CELLS = ROWS * COLS
F32, BF16 = jnp.float32, jnp.bfloat16


def call(body, outs, args, scratch=(), flops=0, after=(), anywhere=False, limit=24):
    used, late = (len(args), len(after))
    inner = body
    if late:
        def inner(*refs):
            body(*refs[:used], *refs[used + late :])
    args = [*args, *after]
    space = pltpu.HBM if anywhere else pltpu.VMEM
    moved = sum(math.prod(a.shape) * a.dtype.itemsize for a in (*args, *outs))
    return pl.pallas_call(
        inner,
        out_shape=tuple(outs),
        in_specs=[pl.BlockSpec(memory_space=space)] * used
        + [pl.BlockSpec(memory_space=pl.ANY)] * late,
        out_specs=tuple(pl.BlockSpec(memory_space=pltpu.VMEM) for _ in outs),
        scratch_shapes=list(scratch),
        compiler_params=pltpu.CompilerParams(vmem_limit_bytes=limit << 20),
        cost_estimate=pl.CostEstimate(flops=flops, bytes_accessed=moved, transcendentals=0),
    )(*args)


def shape(dims, dtype):
    return jax.ShapeDtypeStruct(dims, dtype)


def cells_to_lanes(value, spare):
    count = value.shape[0]
    spare[...] = value[...].astype(F32).reshape(count * ROWS, COLS)
    rows = [spare[pl.ds(h, count, stride=ROWS), :] for h in range(ROWS)]
    return jnp.concatenate(rows, axis=1).astype(BF16)


def lanes_to_cells(value, spare):
    count = value.shape[0]
    for h in range(ROWS):
        spare[pl.ds(h, count, stride=ROWS), :] = value[:, h * COLS : (h + 1) * COLS]
    return spare[...].reshape(count, 1, ROWS, COLS).astype(BF16)


def from_row(value, step):
    if step == 0:
        return value
    gap = jnp.zeros((value.shape[0], COLS), value.dtype)
    if step > 0:
        return jnp.concatenate([value[:, COLS:], gap], axis=1)
    return jnp.concatenate([gap, value[:, :-COLS]], axis=1)


def from_col(value, step):
    if step == 0:
        return value
    lane = lax.broadcasted_iota(jnp.int32, (value.shape[0], COLS), 1)
    keep = lane != (COLS - 1 if step > 0 else 0)
    parts = []
    for h in range(ROWS):
        part = value[:, h * COLS : (h + 1) * COLS].astype(F32)
        part = pltpu.roll(part, (-step) % COLS, axis=1)
        parts.append(jnp.where(keep, part, 0.0).astype(value.dtype))
    return jnp.concatenate(parts, axis=1)


def pack_body(
    volume, grad, bias, volume_out, plane_out, bias_out, here_v, here_g, here_b, spare_v, spare_g, sems
):
    copy_g = pltpu.make_async_copy(grad, here_g, sems.at[0])
    copy_v = pltpu.make_async_copy(volume, here_v, sems.at[1])
    copy_b = pltpu.make_async_copy(bias, here_b, sems.at[2])
    copy_v.start()
    copy_g.start()
    copy_b.start()
    copy_v.wait()
    flat = cells_to_lanes(here_v, spare_v)
    for k in range(volume_out.shape[0]):
        volume_out[k] = flat
    plane_out[16:24] = flat
    copy_g.wait()
    plane_out[0:16] = cells_to_lanes(here_g, spare_g)
    copy_b.wait()
    row = lax.broadcasted_iota(jnp.int32, (16, 16), 0)
    lane = lax.broadcasted_iota(jnp.int32, (16, 16), 1)
    column = jnp.sum(jnp.where(row == lane, here_b[...], 0.0), axis=1, keepdims=True)
    bias_out[...] = jnp.broadcast_to(column, (16, COLS))


def kernel_grad_body(volume, after, here, before, out):
    left = jnp.concatenate(
        [from_row(g[0:16], 1 - b) for g in (after, here, before) for b in range(3)], axis=0
    )
    right = jnp.concatenate([from_col(volume[...], c - 1) for c in range(3)], axis=0)
    sums = lax.dot_general(left, right, (((1,), (1,)), ((), ())), preferred_element_type=F32)
    out[0:144] = sums[:, 0:128]
    out[144:216] = jnp.concatenate([sums[0:72, 128:192], sums[72:144, 128:192]], axis=1)
    total = jnp.sum(here[0:16].astype(F32), axis=1, keepdims=True)
    wide = jnp.broadcast_to(total, (16, 128))
    row = lax.broadcasted_iota(jnp.int32, (16, 128), 0)
    lane = lax.broadcasted_iota(jnp.int32, (16, 128), 1)
    across = jnp.sum(jnp.where(row == lane, wide, 0.0), axis=0, keepdims=True)
    out[216:224] = jnp.broadcast_to(across, (8, 128))
    out[224:] = jnp.zeros((out.shape[0] - 224, 128), F32)


def sum_body(factor, parts, out):
    total = parts[0]
    for k in range(1, parts.shape[0]):
        total = total + parts[k]
    if factor is not None:
        total = total * factor
    for k in range(out.shape[0]):
        out[k] = total


def unpack_body(flat, kernel_out, bias_out):
    for a in range(3):
        for b in range(3):
            for half in range(2):
                r = (a * 3 + b) * 16 + half * 8
                o = slice(half * 8, half * 8 + 8)
                pair = flat[r : r + 8]
                kernel_out[a, b, 0, o] = pair[:, 0:64]
                kernel_out[a, b, 1, o] = pair[:, 64:128]
                if r < 72:
                    kernel_out[a, b, 2, o] = flat[144 + r : 152 + r][:, 0:64]
                else:
                    kernel_out[a, b, 2, o] = flat[72 + r : 80 + r][:, 64:128]
    bias_out[...] = flat[216:217, 0:16]


def input_grad_body(kernel, after, here, before, own, first, second, third, blocks):
    left = jnp.concatenate([kernel[:, b].reshape(144, 64) for b in range(3)], axis=1)
    right = jnp.concatenate(
        [from_col(g[0:16], 1 - c) for g in (after, here, before) for c in range(3)], axis=0
    )
    sums = lax.dot_general(left, right, (((0,), (0,)), ((), ())), preferred_element_type=F32)
    total = sums[64:128]
    total = total + from_row(sums[0:64], 1)
    total = total + from_row(sums[128:192], -1)
    for y in range(4):
        blocks[y] = total[16 * y : 16 * y + 16]
    y = lax.div(lax.axis_index("chan"), 2)
    own[...] = blocks[y]
    for k, out in enumerate((first, second, third)):
        out[0:16], out[16:32] = halves(blocks[lax.rem(y + k + 1, 4)])
        out[32:40] = before[16:24]
        out[40:48] = after[16:24]


def halves(value):
    high = value.astype(BF16)
    return high, (value - high.astype(F32)).astype(BF16)


def join_body(own, first, second, third, before, after, kept, sent):
    chan = lax.axis_index("chan")
    y, odd = lax.div(chan, 2), lax.rem(chan, 2) == 1
    total = own[...]
    for part in (first, second, third):
        total = total + (part[0:16].astype(F32) + part[16:32].astype(F32))
    kept[...] = jnp.where(odd, total[8:16], total[0:8])
    sent[0], sent[1] = halves(jnp.where(odd, total[0:8], total[8:16]))
    sent[2 + 2 * y] = before[16:24]
    sent[3 + 2 * y] = after[16:24]
    for k, part in enumerate((first, second, third)):
        source = lax.rem(y + 3 - k, 4)
        sent[2 + 2 * source] = part[32:40]
        sent[3 + 2 * source] = part[40:48]


def narrow_body(kept, got, out, spare):
    total = kept[...] + (got[0].astype(F32) + got[1].astype(F32))
    out[...] = lanes_to_cells(total, spare)


def feature_body(kernel, bias, here, mine, theirs, out, before, after, spare):
    odd = lax.rem(lax.axis_index("chan"), 2) == 1
    for side, plane in enumerate((before, after)):
        for y in range(4):
            a, b = mine[2 + 2 * y + side].astype(F32), theirs[2 + 2 * y + side].astype(F32)
            plane[16 * y : 16 * y + 8] = jnp.where(odd, b, a).astype(BF16)
            plane[16 * y + 8 : 16 * y + 16] = jnp.where(odd, a, b).astype(BF16)
    left = jnp.concatenate([kernel[a].reshape(144, 64) for a in range(3)], axis=1)
    right = jnp.concatenate([before[...], here[...], after[...]], axis=0)
    sums = jnp.dot(left, right, preferred_element_type=F32)
    total = jnp.concatenate([bias[...]] * ROWS, axis=1)
    for c in range(3):
        part = None
        for b in range(3):
            r = (b * 3 + c) * 16
            term = from_row(sums[r : r + 16], b - 1)
            part = term if part is None else part + term
        total = total + from_col(part, c - 1)
    out[...] = lanes_to_cells(total, spare)


def on_device(volume, kernel, bias, out_grad):
    slabs = X * Z
    groups = lax.axis_size("chan")
    up = [(i, i + 1) for i in range(slabs - 1)]
    down = [(i + 1, i) for i in range(slabs - 1)]
    weights = jnp.transpose(kernel, (0, 1, 2, 4, 3))

    sent, here, column = call(
        pack_body,
        [shape((groups, 8, CELLS), BF16), shape((24, CELLS), BF16), shape((16, COLS), F32)],
        [volume, out_grad, bias.reshape(1, 16)],
        [
            pltpu.VMEM(volume.shape, BF16),
            pltpu.VMEM(out_grad.shape, BF16),
            pltpu.VMEM((1, 16), F32),
            pltpu.VMEM((8 * ROWS, COLS), F32),
            pltpu.VMEM((16 * ROWS, COLS), F32),
            pltpu.SemaphoreType.DMA((3,)),
        ],
        anywhere=True,
        limit=60,
    )
    before = lax.ppermute(here, SLAB, up)
    after = lax.ppermute(here, SLAB, down)
    whole = lax.all_to_all(sent, "chan", 0, 0).reshape(64, CELLS)

    (partial,) = call(
        kernel_grad_body,
        [shape((256, 128), F32)],
        [whole, after, here, before],
        flops=2 * 144 * 192 * CELLS,
    )
    own, *shares = call(
        input_grad_body,
        [shape((16, CELLS), F32)] + [shape((48, CELLS), BF16)] * 3,
        [weights, after, here, before],
        [pltpu.VMEM((4, 16, CELLS), F32)],
        flops=2 * 144 * 192 * CELLS,
    )
    others = [
        lax.ppermute(part, "chan", [(i, (i + 2 * k + 2) % groups) for i in range(groups)])
        for k, part in enumerate(shares)
    ]
    near = X * ZL
    rows = 256 // near
    parts = lax.all_to_all(partial.reshape(near, rows, 128), NEAR, 0, 0)
    (spread,) = call(
        functools.partial(sum_body, None),
        [shape((ZH, rows, 128), F32)],
        [parts],
        after=[others[0]],
    )
    parts = lax.all_to_all(spread, "zh", 0, 0)
    kept, sent = call(
        join_body,
        [shape((8, CELLS), F32), shape((10, 8, CELLS), BF16)],
        [own, *others, before, after],
        after=[spread],
    )
    got = lax.ppermute(sent, "chan", [(i, i ^ 1) for i in range(groups)])
    factor = 1.0 / math.sqrt(slabs * CELLS)
    (spread,) = call(
        functools.partial(sum_body, factor),
        [shape((near, rows, 128), F32)],
        [parts],
        after=[kept],
    )
    flat = lax.all_to_all(spread, NEAR, 0, 0).reshape(256, 128)
    kernel_out, bias_out = call(
        unpack_body, [shape((3, 3, 3, 16, 64), F32), shape((1, 16), F32)], [flat]
    )

    (input_grad,) = call(
        narrow_body,
        [shape((8, 1, ROWS, COLS), BF16)],
        [kept, got],
        [pltpu.VMEM((8 * ROWS, COLS), F32)],
    )

    (feature,) = call(
        feature_body,
        [shape((16, 1, ROWS, COLS), BF16)],
        [weights, column, whole, sent, got],
        [
            pltpu.VMEM((64, CELLS), BF16),
            pltpu.VMEM((64, CELLS), BF16),
            pltpu.VMEM((16 * ROWS, COLS), F32),
        ],
        flops=2 * 144 * 192 * CELLS,
    )
    return (
        feature,
        input_grad,
        jnp.transpose(kernel_out, (0, 1, 2, 4, 3)),
        bias_out.reshape(16),
    )


def solution(mesh):
    split = Mesh(mesh.devices.reshape(X, ZH, ZL, -1), ("x", "zh", "zl", "chan"))
    in_specs = (
        P("chan", SLAB, None, None),
        P(None, None, None, None, "chan"),
        P("chan"),
        P("chan", SLAB, None, None),
    )
    out_specs = (
        P("chan", SLAB, None, None),
        P("chan", SLAB, None, None),
        P(None, None, None, None, "chan"),
        P("chan"),
    )
    return jax.shard_map(
        on_device, mesh=split, in_specs=in_specs, out_specs=out_specs, check_vma=False
    )
```

```python
import functools
import math

import jax
import jax.numpy as jnp
from jax import lax
from jax.experimental import pallas as pl
from jax.experimental.pallas import tpu as pltpu
from jax.sharding import Mesh, PartitionSpec as P

X, Z = 4, 32
ZL = 4
ZH = Z // ZL
SLAB = ("x", "zh", "zl")
NEAR = ("x", "zl")
ROWS, COLS = 16, 128
CELLS = ROWS * COLS
F32, BF16 = jnp.float32, jnp.bfloat16


def call(body, outs, args, scratch=(), flops=0, after=(), anywhere=False, limit=24):
    used, late = (len(args), len(after))
    inner = body
    if late:
        def inner(*refs):
            body(*refs[:used], *refs[used + late :])
    args = [*args, *after]
    space = pltpu.HBM if anywhere else pltpu.VMEM
    moved = sum(math.prod(a.shape) * a.dtype.itemsize for a in (*args, *outs))
    return pl.pallas_call(
        inner,
        out_shape=tuple(outs),
        in_specs=[pl.BlockSpec(memory_space=space)] * used
        + [pl.BlockSpec(memory_space=pl.ANY)] * late,
        out_specs=tuple(pl.BlockSpec(memory_space=pltpu.VMEM) for _ in outs),
        scratch_shapes=list(scratch),
        compiler_params=pltpu.CompilerParams(vmem_limit_bytes=limit << 20),
        cost_estimate=pl.CostEstimate(flops=flops, bytes_accessed=moved, transcendentals=0),
    )(*args)


def shape(dims, dtype):
    return jax.ShapeDtypeStruct(dims, dtype)


def cells_to_lanes(value, spare):
    count = value.shape[0]
    spare[...] = value[...].astype(F32).reshape(count * ROWS, COLS)
    rows = [spare[pl.ds(h, count, stride=ROWS), :] for h in range(ROWS)]
    return jnp.concatenate(rows, axis=1).astype(BF16)


def lanes_to_cells(value, spare):
    count = value.shape[0]
    for h in range(ROWS):
        spare[pl.ds(h, count, stride=ROWS), :] = value[:, h * COLS : (h + 1) * COLS]
    return spare[...].reshape(count, 1, ROWS, COLS).astype(BF16)


def from_row(value, step):
    if step == 0:
        return value
    gap = jnp.zeros((value.shape[0], COLS), value.dtype)
    if step > 0:
        return jnp.concatenate([value[:, COLS:], gap], axis=1)
    return jnp.concatenate([gap, value[:, :-COLS]], axis=1)


def from_col(value, step):
    if step == 0:
        return value
    lane = lax.broadcasted_iota(jnp.int32, (value.shape[0], COLS), 1)
    keep = lane != (COLS - 1 if step > 0 else 0)
    parts = []
    for h in range(ROWS):
        part = value[:, h * COLS : (h + 1) * COLS].astype(F32)
        part = pltpu.roll(part, (-step) % COLS, axis=1)
        parts.append(jnp.where(keep, part, 0.0).astype(value.dtype))
    return jnp.concatenate(parts, axis=1)


def pack_body(
    volume, grad, bias, volume_out, plane_out, bias_out, here_v, here_g, here_b, spare_v, spare_g, sems
):
    copy_g = pltpu.make_async_copy(grad, here_g, sems.at[0])
    copy_v = pltpu.make_async_copy(volume, here_v, sems.at[1])
    copy_b = pltpu.make_async_copy(bias, here_b, sems.at[2])
    copy_v.start()
    copy_g.start()
    copy_b.start()
    copy_v.wait()
    flat = cells_to_lanes(here_v, spare_v)
    for k in range(volume_out.shape[0]):
        volume_out[k] = flat
    plane_out[16:24] = flat
    copy_g.wait()
    plane_out[0:16] = cells_to_lanes(here_g, spare_g)
    copy_b.wait()
    row = lax.broadcasted_iota(jnp.int32, (16, 16), 0)
    lane = lax.broadcasted_iota(jnp.int32, (16, 16), 1)
    column = jnp.sum(jnp.where(row == lane, here_b[...], 0.0), axis=1, keepdims=True)
    bias_out[...] = jnp.broadcast_to(column, (16, COLS))


def kernel_grad_body(volume, after, here, before, out):
    left = jnp.concatenate(
        [from_row(g[0:16], 1 - b) for g in (after, here, before) for b in range(3)], axis=0
    )
    right = jnp.concatenate([from_col(volume[...], c - 1) for c in range(3)], axis=0)
    sums = lax.dot_general(left, right, (((1,), (1,)), ((), ())), preferred_element_type=F32)
    out[0:144] = sums[:, 0:128]
    out[144:216] = jnp.concatenate([sums[0:72, 128:192], sums[72:144, 128:192]], axis=1)
    total = jnp.sum(here[0:16].astype(F32), axis=1, keepdims=True)
    wide = jnp.broadcast_to(total, (16, 128))
    row = lax.broadcasted_iota(jnp.int32, (16, 128), 0)
    lane = lax.broadcasted_iota(jnp.int32, (16, 128), 1)
    across = jnp.sum(jnp.where(row == lane, wide, 0.0), axis=0, keepdims=True)
    out[216:224] = jnp.broadcast_to(across, (8, 128))
    out[224:] = jnp.zeros((out.shape[0] - 224, 128), F32)


def sum_body(factor, parts, out):
    total = parts[0]
    for k in range(1, parts.shape[0]):
        total = total + parts[k]
    if factor is not None:
        total = total * factor
    for k in range(out.shape[0]):
        out[k] = total


def unpack_body(flat, kernel_out, bias_out):
    for a in range(3):
        for b in range(3):
            for half in range(2):
                r = (a * 3 + b) * 16 + half * 8
                o = slice(half * 8, half * 8 + 8)
                pair = flat[r : r + 8]
                kernel_out[a, b, 0, o] = pair[:, 0:64]
                kernel_out[a, b, 1, o] = pair[:, 64:128]
                if r < 72:
                    kernel_out[a, b, 2, o] = flat[144 + r : 152 + r][:, 0:64]
                else:
                    kernel_out[a, b, 2, o] = flat[72 + r : 80 + r][:, 64:128]
    bias_out[...] = flat[216:217, 0:16]


def input_grad_body(kernel, after, here, before, own, first, second, third, blocks):
    left = jnp.concatenate([kernel[:, b].reshape(144, 64) for b in range(3)], axis=1)
    right = jnp.concatenate(
        [from_col(g[0:16], 1 - c) for g in (after, here, before) for c in range(3)], axis=0
    )
    sums = lax.dot_general(left, right, (((0,), (0,)), ((), ())), preferred_element_type=F32)
    total = sums[64:128]
    total = total + from_row(sums[0:64], 1)
    total = total + from_row(sums[128:192], -1)
    for y in range(4):
        blocks[y] = total[16 * y : 16 * y + 16]
    y = lax.div(lax.axis_index("chan"), 2)
    own[...] = blocks[y]
    for k, out in enumerate((first, second, third)):
        out[0:16], out[16:32] = halves(blocks[lax.rem(y + k + 1, 4)])
        out[32:40] = before[16:24]
        out[40:48] = after[16:24]


def halves(value):
    high = value.astype(BF16)
    return high, (value - high.astype(F32)).astype(BF16)


def join_body(own, first, second, third, before, after, kept, sent):
    chan = lax.axis_index("chan")
    y, odd = lax.div(chan, 2), lax.rem(chan, 2) == 1
    total = own[...]
    for part in (first, second, third):
        total = total + (part[0:16].astype(F32) + part[16:32].astype(F32))
    kept[...] = jnp.where(odd, total[8:16], total[0:8])
    sent[0], sent[1] = halves(jnp.where(odd, total[0:8], total[8:16]))
    sent[2 + 2 * y] = before[16:24]
    sent[3 + 2 * y] = after[16:24]
    for k, part in enumerate((first, second, third)):
        source = lax.rem(y + 3 - k, 4)
        sent[2 + 2 * source] = part[32:40]
        sent[3 + 2 * source] = part[40:48]


def narrow_body(kept, got, out, spare):
    total = kept[...] + (got[0].astype(F32) + got[1].astype(F32))
    out[...] = lanes_to_cells(total, spare)


def feature_body(kernel, bias, here, mine, theirs, out, before, after, spare):
    odd = lax.rem(lax.axis_index("chan"), 2) == 1
    for side, plane in enumerate((before, after)):
        for y in range(4):
            a, b = mine[2 + 2 * y + side].astype(F32), theirs[2 + 2 * y + side].astype(F32)
            plane[16 * y : 16 * y + 8] = jnp.where(odd, b, a).astype(BF16)
            plane[16 * y + 8 : 16 * y + 16] = jnp.where(odd, a, b).astype(BF16)
    left = jnp.concatenate([kernel[a].reshape(144, 64) for a in range(3)], axis=1)
    right = jnp.concatenate([before[...], here[...], after[...]], axis=0)
    sums = jnp.dot(left, right, preferred_element_type=F32)
    total = jnp.concatenate([bias[...]] * ROWS, axis=1)
    for c in range(3):
        part = None
        for b in range(3):
            r = (b * 3 + c) * 16
            term = from_row(sums[r : r + 16], b - 1)
            part = term if part is None else part + term
        total = total + from_col(part, c - 1)
    out[...] = lanes_to_cells(total, spare)


def on_device(volume, kernel, bias, out_grad):
    slabs = X * Z
    groups = lax.axis_size("chan")
    up = [(i, i + 1) for i in range(slabs - 1)]
    down = [(i + 1, i) for i in range(slabs - 1)]
    weights = jnp.transpose(kernel, (0, 1, 2, 4, 3))

    sent, here, column = call(
        pack_body,
        [shape((groups, 8, CELLS), BF16), shape((24, CELLS), BF16), shape((16, COLS), F32)],
        [volume, out_grad, bias.reshape(1, 16)],
        [
            pltpu.VMEM(volume.shape, BF16),
            pltpu.VMEM(out_grad.shape, BF16),
            pltpu.VMEM((1, 16), F32),
            pltpu.VMEM((8 * ROWS, COLS), F32),
            pltpu.VMEM((16 * ROWS, COLS), F32),
            pltpu.SemaphoreType.DMA((3,)),
        ],
        anywhere=True,
        limit=60,
    )
    before = lax.ppermute(here, SLAB, up)
    after = lax.ppermute(here, SLAB, down)
    whole = lax.all_to_all(sent, "chan", 0, 0).reshape(64, CELLS)

    (partial,) = call(
        kernel_grad_body,
        [shape((256, 128), F32)],
        [whole, after, here, before],
        flops=2 * 144 * 192 * CELLS,
    )
    own, *shares = call(
        input_grad_body,
        [shape((16, CELLS), F32)] + [shape((48, CELLS), BF16)] * 3,
        [weights, after, here, before],
        [pltpu.VMEM((4, 16, CELLS), F32)],
        flops=2 * 144 * 192 * CELLS,
    )
    others = [
        lax.ppermute(part, "chan", [(i, (i + 2 * k + 2) % groups) for i in range(groups)])
        for k, part in enumerate(shares)
    ]
    near = X * ZL
    rows = 256 // near
    parts = lax.all_to_all(partial.reshape(near, rows, 128), NEAR, 0, 0)
    (spread,) = call(
        functools.partial(sum_body, None),
        [shape((ZH, rows, 128), F32)],
        [parts],
    )
    parts = lax.all_to_all(spread, "zh", 0, 0)
    kept, sent = call(
        join_body,
        [shape((8, CELLS), F32), shape((10, 8, CELLS), BF16)],
        [own, *others, before, after],
        after=[spread],
    )
    got = lax.ppermute(sent, "chan", [(i, i ^ 1) for i in range(groups)])
    factor = 1.0 / math.sqrt(slabs * CELLS)
    (spread,) = call(
        functools.partial(sum_body, factor),
        [shape((near, rows, 128), F32)],
        [parts],
        after=[kept],
    )
    flat = lax.all_to_all(spread, NEAR, 0, 0).reshape(256, 128)
    kernel_out, bias_out = call(
        unpack_body, [shape((3, 3, 3, 16, 64), F32), shape((1, 16), F32)], [flat]
    )

    (input_grad,) = call(
        narrow_body,
        [shape((8, 1, ROWS, COLS), BF16)],
        [kept, got],
        [pltpu.VMEM((8 * ROWS, COLS), F32)],
    )

    (feature,) = call(
        feature_body,
        [shape((16, 1, ROWS, COLS), BF16)],
        [weights, column, whole, sent, got],
        [
            pltpu.VMEM((64, CELLS), BF16),
            pltpu.VMEM((64, CELLS), BF16),
            pltpu.VMEM((16 * ROWS, COLS), F32),
        ],
        flops=2 * 144 * 192 * CELLS,
    )
    return (
        feature,
        input_grad,
        jnp.transpose(kernel_out, (0, 1, 2, 4, 3)),
        bias_out.reshape(16),
    )


def solution(mesh):
    split = Mesh(mesh.devices.reshape(X, ZH, ZL, -1), ("x", "zh", "zl", "chan"))
    in_specs = (
        P("chan", SLAB, None, None),
        P(None, None, None, None, "chan"),
        P("chan"),
        P("chan", SLAB, None, None),
    )
    out_specs = (
        P("chan", SLAB, None, None),
        P("chan", SLAB, None, None),
        P(None, None, None, None, "chan"),
        P("chan"),
    )
    return jax.shard_map(
        on_device, mesh=split, in_specs=in_specs, out_specs=out_specs, check_vma=False
    )
```

```python
import functools
import math

import jax
import jax.numpy as jnp
from jax import lax
from jax.experimental import pallas as pl
from jax.experimental.pallas import tpu as pltpu
from jax.sharding import PartitionSpec as P

X, Z = 4, 32
ZL = 4
ZH = Z // ZL
SLAB = "slab"
FAR_ORDER = [(h + ZH // 2) % ZH for h in range(ZH)]
NEAR_ORDER = [(k + ZL // 2) % ZL for k in range(ZL)]
FAR = [[x * Z + h * ZL + k for h in FAR_ORDER] for x in range(X) for k in range(ZL)]
NEAR = [[x * Z + h * ZL + k for k in NEAR_ORDER for x in range(X)] for h in range(ZH)]
ROWS, COLS = 16, 128
CELLS = ROWS * COLS
F32, BF16 = jnp.float32, jnp.bfloat16


def call(body, outs, args, scratch=(), flops=0, after=(), anywhere=False, limit=24):
    used, late = (len(args), len(after))
    inner = body
    if late:
        def inner(*refs):
            body(*refs[:used], *refs[used + late :])
    args = [*args, *after]
    space = pltpu.HBM if anywhere else pltpu.VMEM
    moved = sum(math.prod(a.shape) * a.dtype.itemsize for a in (*args, *outs))
    return pl.pallas_call(
        inner,
        out_shape=tuple(outs),
        in_specs=[pl.BlockSpec(memory_space=space)] * used
        + [pl.BlockSpec(memory_space=pl.ANY)] * late,
        out_specs=tuple(pl.BlockSpec(memory_space=pltpu.VMEM) for _ in outs),
        scratch_shapes=list(scratch),
        compiler_params=pltpu.CompilerParams(vmem_limit_bytes=limit << 20),
        cost_estimate=pl.CostEstimate(flops=flops, bytes_accessed=moved, transcendentals=0),
    )(*args)


def shape(dims, dtype):
    return jax.ShapeDtypeStruct(dims, dtype)


def cells_to_lanes(value, spare):
    count = value.shape[0]
    spare[...] = value[...].astype(F32).reshape(count * ROWS, COLS)
    rows = [spare[pl.ds(h, count, stride=ROWS), :] for h in range(ROWS)]
    return jnp.concatenate(rows, axis=1).astype(BF16)


def lanes_to_cells(value, spare):
    count = value.shape[0]
    for h in range(ROWS):
        spare[pl.ds(h, count, stride=ROWS), :] = value[:, h * COLS : (h + 1) * COLS]
    return spare[...].reshape(count, 1, ROWS, COLS).astype(BF16)


def from_row(value, step):
    if step == 0:
        return value
    gap = jnp.zeros((value.shape[0], COLS), value.dtype)
    if step > 0:
        return jnp.concatenate([value[:, COLS:], gap], axis=1)
    return jnp.concatenate([gap, value[:, :-COLS]], axis=1)


def from_col(value, step):
    if step == 0:
        return value
    lane = lax.broadcasted_iota(jnp.int32, (value.shape[0], COLS), 1)
    keep = lane != (COLS - 1 if step > 0 else 0)
    parts = []
    for h in range(ROWS):
        part = value[:, h * COLS : (h + 1) * COLS].astype(F32)
        part = pltpu.roll(part, (-step) % COLS, axis=1)
        parts.append(jnp.where(keep, part, 0.0).astype(value.dtype))
    return jnp.concatenate(parts, axis=1)


def pack_body(
    volume, grad, bias, volume_out, plane_out, bias_out, here_v, here_g, here_b, spare_v, spare_g, sems
):
    copy_g = pltpu.make_async_copy(grad, here_g, sems.at[0])
    copy_v = pltpu.make_async_copy(volume, here_v, sems.at[1])
    copy_b = pltpu.make_async_copy(bias, here_b, sems.at[2])
    copy_v.start()
    copy_g.start()
    copy_b.start()
    copy_v.wait()
    flat = cells_to_lanes(here_v, spare_v)
    for k in range(volume_out.shape[0]):
        volume_out[k] = flat
    plane_out[16:24] = flat
    copy_g.wait()
    plane_out[0:16] = cells_to_lanes(here_g, spare_g)
    copy_b.wait()
    row = lax.broadcasted_iota(jnp.int32, (16, 16), 0)
    lane = lax.broadcasted_iota(jnp.int32, (16, 16), 1)
    column = jnp.sum(jnp.where(row == lane, here_b[...], 0.0), axis=1, keepdims=True)
    bias_out[...] = jnp.broadcast_to(column, (16, COLS))


def kernel_grad_body(volume, after, here, before, out):
    left = jnp.concatenate(
        [from_row(g[0:16], 1 - b) for g in (after, here, before) for b in range(3)], axis=0
    )
    right = jnp.concatenate([from_col(volume[...], c - 1) for c in range(3)], axis=0)
    sums = lax.dot_general(left, right, (((1,), (1,)), ((), ())), preferred_element_type=F32)
    out[0:144] = sums[:, 0:128]
    out[144:216] = jnp.concatenate([sums[0:72, 128:192], sums[72:144, 128:192]], axis=1)
    total = jnp.sum(here[0:16].astype(F32), axis=1, keepdims=True)
    wide = jnp.broadcast_to(total, (16, 128))
    row = lax.broadcasted_iota(jnp.int32, (16, 128), 0)
    lane = lax.broadcasted_iota(jnp.int32, (16, 128), 1)
    across = jnp.sum(jnp.where(row == lane, wide, 0.0), axis=0, keepdims=True)
    out[216:224] = jnp.broadcast_to(across, (8, 128))
    out[224:] = jnp.zeros((out.shape[0] - 224, 128), F32)


def sum_body(factor, parts, out):
    total = parts[0]
    for k in range(1, parts.shape[0]):
        total = total + parts[k]
    if factor is not None:
        total = total * factor
    for k in range(out.shape[0]):
        out[k] = total


def unpack_body(flat, kernel_out, bias_out):
    for a in range(3):
        for b in range(3):
            for half in range(2):
                r = (a * 3 + b) * 16 + half * 8
                o = slice(half * 8, half * 8 + 8)
                pair = flat[r : r + 8]
                kernel_out[a, b, 0, o] = pair[:, 0:64]
                kernel_out[a, b, 1, o] = pair[:, 64:128]
                if r < 72:
                    kernel_out[a, b, 2, o] = flat[144 + r : 152 + r][:, 0:64]
                else:
                    kernel_out[a, b, 2, o] = flat[72 + r : 80 + r][:, 64:128]
    bias_out[...] = flat[216:217, 0:16]


def input_grad_body(kernel, after, here, before, own, first, second, third, blocks):
    left = jnp.concatenate([kernel[:, b].reshape(144, 64) for b in range(3)], axis=1)
    right = jnp.concatenate(
        [from_col(g[0:16], 1 - c) for g in (after, here, before) for c in range(3)], axis=0
    )
    sums = lax.dot_general(left, right, (((0,), (0,)), ((), ())), preferred_element_type=F32)
    total = sums[64:128]
    total = total + from_row(sums[0:64], 1)
    total = total + from_row(sums[128:192], -1)
    for y in range(4):
        blocks[y] = total[16 * y : 16 * y + 16]
    y = lax.div(lax.axis_index("chan"), 2)
    own[...] = blocks[y]
    for k, out in enumerate((first, second, third)):
        out[0:16], out[16:32] = halves(blocks[lax.rem(y + k + 1, 4)])
        out[32:40] = before[16:24]
        out[40:48] = after[16:24]


def halves(value):
    high = value.astype(BF16)
    return high, (value - high.astype(F32)).astype(BF16)


def join_body(own, first, second, third, before, after, kept, sent):
    chan = lax.axis_index("chan")
    y, odd = lax.div(chan, 2), lax.rem(chan, 2) == 1
    total = own[...]
    for part in (first, second, third):
        total = total + (part[0:16].astype(F32) + part[16:32].astype(F32))
    kept[...] = jnp.where(odd, total[8:16], total[0:8])
    sent[0], sent[1] = halves(jnp.where(odd, total[0:8], total[8:16]))
    sent[2 + 2 * y] = before[16:24]
    sent[3 + 2 * y] = after[16:24]
    for k, part in enumerate((first, second, third)):
        source = lax.rem(y + 3 - k, 4)
        sent[2 + 2 * source] = part[32:40]
        sent[3 + 2 * source] = part[40:48]


def narrow_body(kept, got, out, spare):
    total = kept[...] + (got[0].astype(F32) + got[1].astype(F32))
    out[...] = lanes_to_cells(total, spare)


def feature_body(kernel, bias, here, mine, theirs, out, before, after, spare):
    odd = lax.rem(lax.axis_index("chan"), 2) == 1
    for side, plane in enumerate((before, after)):
        for y in range(4):
            a, b = mine[2 + 2 * y + side].astype(F32), theirs[2 + 2 * y + side].astype(F32)
            plane[16 * y : 16 * y + 8] = jnp.where(odd, b, a).astype(BF16)
            plane[16 * y + 8 : 16 * y + 16] = jnp.where(odd, a, b).astype(BF16)
    left = jnp.concatenate([kernel[a].reshape(144, 64) for a in range(3)], axis=1)
    right = jnp.concatenate([before[...], here[...], after[...]], axis=0)
    sums = jnp.dot(left, right, preferred_element_type=F32)
    total = jnp.concatenate([bias[...]] * ROWS, axis=1)
    for c in range(3):
        part = None
        for b in range(3):
            r = (b * 3 + c) * 16
            term = from_row(sums[r : r + 16], b - 1)
            part = term if part is None else part + term
        total = total + from_col(part, c - 1)
    out[...] = lanes_to_cells(total, spare)


def on_device(volume, kernel, bias, out_grad):
    slabs = X * Z
    groups = lax.axis_size("chan")
    up = [(i, i + 1) for i in range(slabs - 1)]
    down = [(i + 1, i) for i in range(slabs - 1)]
    weights = jnp.transpose(kernel, (0, 1, 2, 4, 3))

    sent, here, column = call(
        pack_body,
        [shape((groups, 8, CELLS), BF16), shape((24, CELLS), BF16), shape((16, COLS), F32)],
        [volume, out_grad, bias.reshape(1, 16)],
        [
            pltpu.VMEM(volume.shape, BF16),
            pltpu.VMEM(out_grad.shape, BF16),
            pltpu.VMEM((1, 16), F32),
            pltpu.VMEM((8 * ROWS, COLS), F32),
            pltpu.VMEM((16 * ROWS, COLS), F32),
            pltpu.SemaphoreType.DMA((3,)),
        ],
        anywhere=True,
        limit=60,
    )
    before = lax.ppermute(here, SLAB, up)
    after = lax.ppermute(here, SLAB, down)
    whole = lax.all_to_all(sent, "chan", 0, 0).reshape(64, CELLS)

    (partial,) = call(
        kernel_grad_body,
        [shape((256, 128), F32)],
        [whole, after, here, before],
        flops=2 * 144 * 192 * CELLS,
    )
    own, *shares = call(
        input_grad_body,
        [shape((16, CELLS), F32)] + [shape((48, CELLS), BF16)] * 3,
        [weights, after, here, before],
        [pltpu.VMEM((4, 16, CELLS), F32)],
        flops=2 * 144 * 192 * CELLS,
    )
    others = [
        lax.ppermute(part, "chan", [(i, (i + 2 * k + 2) % groups) for i in range(groups)])
        for k, part in enumerate(shares)
    ]
    near = X * ZL
    rows = 256 // near
    parts = lax.all_to_all(
        partial.reshape(near, rows, 128), SLAB, 0, 0, axis_index_groups=NEAR
    )
    (spread,) = call(
        functools.partial(sum_body, None),
        [shape((ZH, rows, 128), F32)],
        [parts],
    )
    parts = lax.all_to_all(spread, SLAB, 0, 0, axis_index_groups=FAR)
    kept, sent = call(
        join_body,
        [shape((8, CELLS), F32), shape((10, 8, CELLS), BF16)],
        [own, *others, before, after],
        after=[spread],
    )
    got = lax.ppermute(sent, "chan", [(i, i ^ 1) for i in range(groups)])
    factor = 1.0 / math.sqrt(slabs * CELLS)
    (spread,) = call(
        functools.partial(sum_body, factor),
        [shape((near, rows, 128), F32)],
        [parts],
        after=[kept],
    )
    flat = lax.all_to_all(spread, SLAB, 0, 0, axis_index_groups=NEAR).reshape(256, 128)
    kernel_out, bias_out = call(
        unpack_body, [shape((3, 3, 3, 16, 64), F32), shape((1, 16), F32)], [flat]
    )

    (input_grad,) = call(
        narrow_body,
        [shape((8, 1, ROWS, COLS), BF16)],
        [kept, got],
        [pltpu.VMEM((8 * ROWS, COLS), F32)],
    )

    (feature,) = call(
        feature_body,
        [shape((16, 1, ROWS, COLS), BF16)],
        [weights, column, whole, sent, got],
        [
            pltpu.VMEM((64, CELLS), BF16),
            pltpu.VMEM((64, CELLS), BF16),
            pltpu.VMEM((16 * ROWS, COLS), F32),
        ],
        flops=2 * 144 * 192 * CELLS,
    )
    return (
        feature,
        input_grad,
        jnp.transpose(kernel_out, (0, 1, 2, 4, 3)),
        bias_out.reshape(16),
    )


def solution(mesh):
    in_specs = (
        P("chan", SLAB, None, None),
        P(None, None, None, None, "chan"),
        P("chan"),
        P("chan", SLAB, None, None),
    )
    out_specs = (
        P("chan", SLAB, None, None),
        P("chan", SLAB, None, None),
        P(None, None, None, None, "chan"),
        P("chan"),
    )
    return jax.shard_map(
        on_device, mesh=mesh, in_specs=in_specs, out_specs=out_specs, check_vma=False
    )
```

```python
import functools
import math

import jax
import jax.numpy as jnp
from jax import lax
from jax.experimental import pallas as pl
from jax.experimental.pallas import tpu as pltpu
from jax.sharding import PartitionSpec as P

X, Z = 4, 32
ZL = 4
ZH = Z // ZL
SLAB = "slab"
FAR_ORDER = [(h + ZH * 3 // 4) % ZH for h in range(ZH)]
NEAR_ORDER = [(k + ZL // 2) % ZL for k in range(ZL)]
FAR = [[x * Z + h * ZL + k for h in FAR_ORDER] for x in range(X) for k in range(ZL)]
NEAR = [[x * Z + h * ZL + k for k in NEAR_ORDER for x in range(X)] for h in range(ZH)]
ROWS, COLS = 16, 128
CELLS = ROWS * COLS
F32, BF16 = jnp.float32, jnp.bfloat16


def call(body, outs, args, scratch=(), flops=0, after=(), anywhere=False, limit=24):
    used, late = (len(args), len(after))
    inner = body
    if late:
        def inner(*refs):
            body(*refs[:used], *refs[used + late :])
    args = [*args, *after]
    space = pltpu.HBM if anywhere else pltpu.VMEM
    moved = sum(math.prod(a.shape) * a.dtype.itemsize for a in (*args, *outs))
    return pl.pallas_call(
        inner,
        out_shape=tuple(outs),
        in_specs=[pl.BlockSpec(memory_space=space)] * used
        + [pl.BlockSpec(memory_space=pl.ANY)] * late,
        out_specs=tuple(pl.BlockSpec(memory_space=pltpu.VMEM) for _ in outs),
        scratch_shapes=list(scratch),
        compiler_params=pltpu.CompilerParams(vmem_limit_bytes=limit << 20),
        cost_estimate=pl.CostEstimate(flops=flops, bytes_accessed=moved, transcendentals=0),
    )(*args)


def shape(dims, dtype):
    return jax.ShapeDtypeStruct(dims, dtype)


def cells_to_lanes(value, spare):
    count = value.shape[0]
    spare[...] = value[...].astype(F32).reshape(count * ROWS, COLS)
    rows = [spare[pl.ds(h, count, stride=ROWS), :] for h in range(ROWS)]
    return jnp.concatenate(rows, axis=1).astype(BF16)


def lanes_to_cells(value, spare):
    count = value.shape[0]
    for h in range(ROWS):
        spare[pl.ds(h, count, stride=ROWS), :] = value[:, h * COLS : (h + 1) * COLS]
    return spare[...].reshape(count, 1, ROWS, COLS).astype(BF16)


def from_row(value, step):
    if step == 0:
        return value
    gap = jnp.zeros((value.shape[0], COLS), value.dtype)
    if step > 0:
        return jnp.concatenate([value[:, COLS:], gap], axis=1)
    return jnp.concatenate([gap, value[:, :-COLS]], axis=1)


def from_col(value, step):
    if step == 0:
        return value
    lane = lax.broadcasted_iota(jnp.int32, (value.shape[0], COLS), 1)
    keep = lane != (COLS - 1 if step > 0 else 0)
    parts = []
    for h in range(ROWS):
        part = value[:, h * COLS : (h + 1) * COLS].astype(F32)
        part = pltpu.roll(part, (-step) % COLS, axis=1)
        parts.append(jnp.where(keep, part, 0.0).astype(value.dtype))
    return jnp.concatenate(parts, axis=1)


def pack_body(
    volume, grad, bias, volume_out, plane_out, bias_out, here_v, here_g, here_b, spare_v, spare_g, sems
):
    copy_g = pltpu.make_async_copy(grad, here_g, sems.at[0])
    copy_v = pltpu.make_async_copy(volume, here_v, sems.at[1])
    copy_b = pltpu.make_async_copy(bias, here_b, sems.at[2])
    copy_v.start()
    copy_g.start()
    copy_b.start()
    copy_v.wait()
    flat = cells_to_lanes(here_v, spare_v)
    for k in range(volume_out.shape[0]):
        volume_out[k] = flat
    plane_out[16:24] = flat
    copy_g.wait()
    plane_out[0:16] = cells_to_lanes(here_g, spare_g)
    copy_b.wait()
    row = lax.broadcasted_iota(jnp.int32, (16, 16), 0)
    lane = lax.broadcasted_iota(jnp.int32, (16, 16), 1)
    column = jnp.sum(jnp.where(row == lane, here_b[...], 0.0), axis=1, keepdims=True)
    bias_out[...] = jnp.broadcast_to(column, (16, COLS))


def kernel_grad_body(volume, after, here, before, out):
    left = jnp.concatenate(
        [from_row(g[0:16], 1 - b) for g in (after, here, before) for b in range(3)], axis=0
    )
    right = jnp.concatenate([from_col(volume[...], c - 1) for c in range(3)], axis=0)
    sums = lax.dot_general(left, right, (((1,), (1,)), ((), ())), preferred_element_type=F32)
    out[0:144] = sums[:, 0:128]
    out[144:216] = jnp.concatenate([sums[0:72, 128:192], sums[72:144, 128:192]], axis=1)
    total = jnp.sum(here[0:16].astype(F32), axis=1, keepdims=True)
    wide = jnp.broadcast_to(total, (16, 128))
    row = lax.broadcasted_iota(jnp.int32, (16, 128), 0)
    lane = lax.broadcasted_iota(jnp.int32, (16, 128), 1)
    across = jnp.sum(jnp.where(row == lane, wide, 0.0), axis=0, keepdims=True)
    out[216:224] = jnp.broadcast_to(across, (8, 128))
    out[224:] = jnp.zeros((out.shape[0] - 224, 128), F32)


def sum_body(factor, parts, out):
    total = parts[0]
    for k in range(1, parts.shape[0]):
        total = total + parts[k]
    if factor is not None:
        total = total * factor
    for k in range(out.shape[0]):
        out[k] = total


def unpack_body(flat, kernel_out, bias_out):
    for a in range(3):
        for b in range(3):
            for half in range(2):
                r = (a * 3 + b) * 16 + half * 8
                o = slice(half * 8, half * 8 + 8)
                pair = flat[r : r + 8]
                kernel_out[a, b, 0, o] = pair[:, 0:64]
                kernel_out[a, b, 1, o] = pair[:, 64:128]
                if r < 72:
                    kernel_out[a, b, 2, o] = flat[144 + r : 152 + r][:, 0:64]
                else:
                    kernel_out[a, b, 2, o] = flat[72 + r : 80 + r][:, 64:128]
    bias_out[...] = flat[216:217, 0:16]


def input_grad_body(kernel, after, here, before, own, first, second, third, blocks):
    left = jnp.concatenate([kernel[:, b].reshape(144, 64) for b in range(3)], axis=1)
    right = jnp.concatenate(
        [from_col(g[0:16], 1 - c) for g in (after, here, before) for c in range(3)], axis=0
    )
    sums = lax.dot_general(left, right, (((0,), (0,)), ((), ())), preferred_element_type=F32)
    total = sums[64:128]
    total = total + from_row(sums[0:64], 1)
    total = total + from_row(sums[128:192], -1)
    for y in range(4):
        blocks[y] = total[16 * y : 16 * y + 16]
    y = lax.div(lax.axis_index("chan"), 2)
    own[...] = blocks[y]
    for k, out in enumerate((first, second, third)):
        out[0:16], out[16:32] = halves(blocks[lax.rem(y + k + 1, 4)])
        out[32:40] = before[16:24]
        out[40:48] = after[16:24]


def halves(value):
    high = value.astype(BF16)
    return high, (value - high.astype(F32)).astype(BF16)


def join_body(own, first, second, third, before, after, kept, sent):
    chan = lax.axis_index("chan")
    y, odd = lax.div(chan, 2), lax.rem(chan, 2) == 1
    total = own[...]
    for part in (first, second, third):
        total = total + (part[0:16].astype(F32) + part[16:32].astype(F32))
    kept[...] = jnp.where(odd, total[8:16], total[0:8])
    sent[0], sent[1] = halves(jnp.where(odd, total[0:8], total[8:16]))
    sent[2 + 2 * y] = before[16:24]
    sent[3 + 2 * y] = after[16:24]
    for k, part in enumerate((first, second, third)):
        source = lax.rem(y + 3 - k, 4)
        sent[2 + 2 * source] = part[32:40]
        sent[3 + 2 * source] = part[40:48]


def narrow_body(kept, got, out, spare):
    total = kept[...] + (got[0].astype(F32) + got[1].astype(F32))
    out[...] = lanes_to_cells(total, spare)


def feature_body(kernel, bias, here, mine, theirs, out, before, after, spare):
    odd = lax.rem(lax.axis_index("chan"), 2) == 1
    for side, plane in enumerate((before, after)):
        for y in range(4):
            a, b = mine[2 + 2 * y + side].astype(F32), theirs[2 + 2 * y + side].astype(F32)
            plane[16 * y : 16 * y + 8] = jnp.where(odd, b, a).astype(BF16)
            plane[16 * y + 8 : 16 * y + 16] = jnp.where(odd, a, b).astype(BF16)
    left = jnp.concatenate([kernel[a].reshape(144, 64) for a in range(3)], axis=1)
    right = jnp.concatenate([before[...], here[...], after[...]], axis=0)
    sums = jnp.dot(left, right, preferred_element_type=F32)
    total = jnp.concatenate([bias[...]] * ROWS, axis=1)
    for c in range(3):
        part = None
        for b in range(3):
            r = (b * 3 + c) * 16
            term = from_row(sums[r : r + 16], b - 1)
            part = term if part is None else part + term
        total = total + from_col(part, c - 1)
    out[...] = lanes_to_cells(total, spare)


def on_device(volume, kernel, bias, out_grad):
    slabs = X * Z
    groups = lax.axis_size("chan")
    up = [(i, i + 1) for i in range(slabs - 1)]
    down = [(i + 1, i) for i in range(slabs - 1)]
    weights = jnp.transpose(kernel, (0, 1, 2, 4, 3))

    sent, here, column = call(
        pack_body,
        [shape((groups, 8, CELLS), BF16), shape((24, CELLS), BF16), shape((16, COLS), F32)],
        [volume, out_grad, bias.reshape(1, 16)],
        [
            pltpu.VMEM(volume.shape, BF16),
            pltpu.VMEM(out_grad.shape, BF16),
            pltpu.VMEM((1, 16), F32),
            pltpu.VMEM((8 * ROWS, COLS), F32),
            pltpu.VMEM((16 * ROWS, COLS), F32),
            pltpu.SemaphoreType.DMA((3,)),
        ],
        anywhere=True,
        limit=60,
    )
    before = lax.ppermute(here, SLAB, up)
    after = lax.ppermute(here, SLAB, down)
    whole = lax.all_to_all(sent, "chan", 0, 0).reshape(64, CELLS)

    (partial,) = call(
        kernel_grad_body,
        [shape((256, 128), F32)],
        [whole, after, here, before],
        flops=2 * 144 * 192 * CELLS,
    )
    own, *shares = call(
        input_grad_body,
        [shape((16, CELLS), F32)] + [shape((48, CELLS), BF16)] * 3,
        [weights, after, here, before],
        [pltpu.VMEM((4, 16, CELLS), F32)],
        flops=2 * 144 * 192 * CELLS,
    )
    others = [
        lax.ppermute(part, "chan", [(i, (i + 2 * k + 2) % groups) for i in range(groups)])
        for k, part in enumerate(shares)
    ]
    near = X * ZL
    rows = 256 // near
    parts = lax.all_to_all(
        partial.reshape(near, rows, 128), SLAB, 0, 0, axis_index_groups=NEAR
    )
    (spread,) = call(
        functools.partial(sum_body, None),
        [shape((ZH, rows, 128), F32)],
        [parts],
    )
    parts = lax.all_to_all(spread, SLAB, 0, 0, axis_index_groups=FAR)
    kept, sent = call(
        join_body,
        [shape((8, CELLS), F32), shape((10, 8, CELLS), BF16)],
        [own, *others, before, after],
        after=[spread],
    )
    got = lax.ppermute(sent, "chan", [(i, i ^ 1) for i in range(groups)])
    factor = 1.0 / math.sqrt(slabs * CELLS)
    (spread,) = call(
        functools.partial(sum_body, factor),
        [shape((near, rows, 128), F32)],
        [parts],
        after=[kept],
    )
    flat = lax.all_to_all(spread, SLAB, 0, 0, axis_index_groups=NEAR).reshape(256, 128)
    kernel_out, bias_out = call(
        unpack_body, [shape((3, 3, 3, 16, 64), F32), shape((1, 16), F32)], [flat]
    )

    (input_grad,) = call(
        narrow_body,
        [shape((8, 1, ROWS, COLS), BF16)],
        [kept, got],
        [pltpu.VMEM((8 * ROWS, COLS), F32)],
    )

    (feature,) = call(
        feature_body,
        [shape((16, 1, ROWS, COLS), BF16)],
        [weights, column, whole, sent, got],
        [
            pltpu.VMEM((64, CELLS), BF16),
            pltpu.VMEM((64, CELLS), BF16),
            pltpu.VMEM((16 * ROWS, COLS), F32),
        ],
        flops=2 * 144 * 192 * CELLS,
    )
    return (
        feature,
        input_grad,
        jnp.transpose(kernel_out, (0, 1, 2, 4, 3)),
        bias_out.reshape(16),
    )


def solution(mesh):
    in_specs = (
        P("chan", SLAB, None, None),
        P(None, None, None, None, "chan"),
        P("chan"),
        P("chan", SLAB, None, None),
    )
    out_specs = (
        P("chan", SLAB, None, None),
        P("chan", SLAB, None, None),
        P(None, None, None, None, "chan"),
        P("chan"),
    )
    return jax.shard_map(
        on_device, mesh=mesh, in_specs=in_specs, out_specs=out_specs, check_vma=False
    )
```

```python
import functools
import math

import jax
import jax.numpy as jnp
from jax import lax
from jax.experimental import pallas as pl
from jax.experimental.pallas import tpu as pltpu
from jax.sharding import PartitionSpec as P

X, Z = 4, 32
ZL = 4
ZH = Z // ZL
SLAB = "slab"
FAR_ORDER = [(h + ZH * 3 // 4) % ZH for h in range(ZH)]
NEAR_ORDER = [(k + ZL // 2) % ZL for k in range(ZL)]
FAR = [[x * Z + h * ZL + k for h in FAR_ORDER] for x in range(X) for k in range(ZL)]
NEAR = [[x * Z + h * ZL + k for k in NEAR_ORDER for x in range(X)] for h in range(ZH)]
ROWS, COLS = 16, 128
FL = 1 << 34
CELLS = ROWS * COLS
F32, BF16 = jnp.float32, jnp.bfloat16


def call(body, outs, args, scratch=(), flops=0, after=(), anywhere=False, limit=24):
    used, late = (len(args), len(after))
    inner = body
    if late:
        def inner(*refs):
            body(*refs[:used], *refs[used + late :])
    args = [*args, *after]
    space = pltpu.HBM if anywhere else pltpu.VMEM
    moved = sum(math.prod(a.shape) * a.dtype.itemsize for a in (*args, *outs))
    return pl.pallas_call(
        inner,
        out_shape=tuple(outs),
        in_specs=[pl.BlockSpec(memory_space=space)] * used
        + [pl.BlockSpec(memory_space=pl.ANY)] * late,
        out_specs=tuple(pl.BlockSpec(memory_space=pltpu.VMEM) for _ in outs),
        scratch_shapes=list(scratch),
        compiler_params=pltpu.CompilerParams(vmem_limit_bytes=limit << 20),
        cost_estimate=pl.CostEstimate(flops=flops, bytes_accessed=moved, transcendentals=0),
    )(*args)


def shape(dims, dtype):
    return jax.ShapeDtypeStruct(dims, dtype)


def cells_to_lanes(value, spare):
    count = value.shape[0]
    spare[...] = value[...].astype(F32).reshape(count * ROWS, COLS)
    rows = [spare[pl.ds(h, count, stride=ROWS), :] for h in range(ROWS)]
    return jnp.concatenate(rows, axis=1).astype(BF16)


def lanes_to_cells(value, spare):
    count = value.shape[0]
    for h in range(ROWS):
        spare[pl.ds(h, count, stride=ROWS), :] = value[:, h * COLS : (h + 1) * COLS]
    return spare[...].reshape(count, 1, ROWS, COLS).astype(BF16)


def from_row(value, step):
    if step == 0:
        return value
    gap = jnp.zeros((value.shape[0], COLS), value.dtype)
    if step > 0:
        return jnp.concatenate([value[:, COLS:], gap], axis=1)
    return jnp.concatenate([gap, value[:, :-COLS]], axis=1)


def from_col(value, step):
    if step == 0:
        return value
    lane = lax.broadcasted_iota(jnp.int32, (value.shape[0], COLS), 1)
    keep = lane != (COLS - 1 if step > 0 else 0)
    parts = []
    for h in range(ROWS):
        part = value[:, h * COLS : (h + 1) * COLS].astype(F32)
        part = pltpu.roll(part, (-step) % COLS, axis=1)
        parts.append(jnp.where(keep, part, 0.0).astype(value.dtype))
    return jnp.concatenate(parts, axis=1)


def pack_body(
    volume, grad, bias, volume_out, plane_out, bias_out, here_v, here_g, here_b, spare_v, spare_g, sems
):
    copy_g = pltpu.make_async_copy(grad, here_g, sems.at[0])
    copy_v = pltpu.make_async_copy(volume, here_v, sems.at[1])
    copy_b = pltpu.make_async_copy(bias, here_b, sems.at[2])
    copy_v.start()
    copy_g.start()
    copy_b.start()
    copy_v.wait()
    flat = cells_to_lanes(here_v, spare_v)
    for k in range(volume_out.shape[0]):
        volume_out[k] = flat
    plane_out[16:24] = flat
    copy_g.wait()
    plane_out[0:16] = cells_to_lanes(here_g, spare_g)
    copy_b.wait()
    row = lax.broadcasted_iota(jnp.int32, (16, 16), 0)
    lane = lax.broadcasted_iota(jnp.int32, (16, 16), 1)
    column = jnp.sum(jnp.where(row == lane, here_b[...], 0.0), axis=1, keepdims=True)
    bias_out[...] = jnp.broadcast_to(column, (16, COLS))


def kernel_grad_body(volume, after, here, before, out):
    left = jnp.concatenate(
        [from_row(g[0:16], 1 - b) for g in (after, here, before) for b in range(3)], axis=0
    )
    right = jnp.concatenate([from_col(volume[...], c - 1) for c in range(3)], axis=0)
    sums = lax.dot_general(left, right, (((1,), (1,)), ((), ())), preferred_element_type=F32)
    out[0:144] = sums[:, 0:128]
    out[144:216] = jnp.concatenate([sums[0:72, 128:192], sums[72:144, 128:192]], axis=1)
    total = jnp.sum(here[0:16].astype(F32), axis=1, keepdims=True)
    wide = jnp.broadcast_to(total, (16, 128))
    row = lax.broadcasted_iota(jnp.int32, (16, 128), 0)
    lane = lax.broadcasted_iota(jnp.int32, (16, 128), 1)
    across = jnp.sum(jnp.where(row == lane, wide, 0.0), axis=0, keepdims=True)
    out[216:224] = jnp.broadcast_to(across, (8, 128))
    out[224:] = jnp.zeros((out.shape[0] - 224, 128), F32)


def sum_body(factor, parts, out):
    total = parts[0]
    for k in range(1, parts.shape[0]):
        total = total + parts[k]
    if factor is not None:
        total = total * factor
    for k in range(out.shape[0]):
        out[k] = total


def unpack_body(flat, kernel_out, bias_out):
    for a in range(3):
        for b in range(3):
            for half in range(2):
                r = (a * 3 + b) * 16 + half * 8
                o = slice(half * 8, half * 8 + 8)
                pair = flat[r : r + 8]
                kernel_out[a, b, 0, o] = pair[:, 0:64]
                kernel_out[a, b, 1, o] = pair[:, 64:128]
                if r < 72:
                    kernel_out[a, b, 2, o] = flat[144 + r : 152 + r][:, 0:64]
                else:
                    kernel_out[a, b, 2, o] = flat[72 + r : 80 + r][:, 64:128]
    bias_out[...] = flat[216:217, 0:16]


def input_grad_body(kernel, after, here, before, own, first, second, third, blocks):
    left = jnp.concatenate([kernel[:, b].reshape(144, 64) for b in range(3)], axis=1)
    right = jnp.concatenate(
        [from_col(g[0:16], 1 - c) for g in (after, here, before) for c in range(3)], axis=0
    )
    sums = lax.dot_general(left, right, (((0,), (0,)), ((), ())), preferred_element_type=F32)
    total = sums[64:128]
    total = total + from_row(sums[0:64], 1)
    total = total + from_row(sums[128:192], -1)
    for y in range(4):
        blocks[y] = total[16 * y : 16 * y + 16]
    y = lax.div(lax.axis_index("chan"), 2)
    own[...] = blocks[y]
    for k, out in enumerate((first, second, third)):
        out[0:16], out[16:32] = halves(blocks[lax.rem(y + k + 1, 4)])
        out[32:40] = before[16:24]
        out[40:48] = after[16:24]


def halves(value):
    high = value.astype(BF16)
    return high, (value - high.astype(F32)).astype(BF16)


def join_body(own, first, second, third, before, after, kept, sent):
    chan = lax.axis_index("chan")
    y, odd = lax.div(chan, 2), lax.rem(chan, 2) == 1
    total = own[...]
    for part in (first, second, third):
        total = total + (part[0:16].astype(F32) + part[16:32].astype(F32))
    kept[...] = jnp.where(odd, total[8:16], total[0:8])
    sent[0], sent[1] = halves(jnp.where(odd, total[0:8], total[8:16]))
    sent[2 + 2 * y] = before[16:24]
    sent[3 + 2 * y] = after[16:24]
    for k, part in enumerate((first, second, third)):
        source = lax.rem(y + 3 - k, 4)
        sent[2 + 2 * source] = part[32:40]
        sent[3 + 2 * source] = part[40:48]


def feature_body(
    kernel, bias, here, kept, mine, theirs, out, grad_out, before, after, spare, spare_g
):
    total = kept[...] + (theirs[0].astype(F32) + theirs[1].astype(F32))
    grad_out[...] = lanes_to_cells(total, spare_g)
    odd = lax.rem(lax.axis_index("chan"), 2) == 1
    for side, plane in enumerate((before, after)):
        for y in range(4):
            a, b = mine[2 + 2 * y + side].astype(F32), theirs[2 + 2 * y + side].astype(F32)
            plane[16 * y : 16 * y + 8] = jnp.where(odd, b, a).astype(BF16)
            plane[16 * y + 8 : 16 * y + 16] = jnp.where(odd, a, b).astype(BF16)
    left = jnp.concatenate([kernel[a].reshape(144, 64) for a in range(3)], axis=1)
    right = jnp.concatenate([before[...], here[...], after[...]], axis=0)
    sums = jnp.dot(left, right, preferred_element_type=F32)
    total = jnp.concatenate([bias[...]] * ROWS, axis=1)
    for c in range(3):
        part = None
        for b in range(3):
            r = (b * 3 + c) * 16
            term = from_row(sums[r : r + 16], b - 1)
            part = term if part is None else part + term
        total = total + from_col(part, c - 1)
    out[...] = lanes_to_cells(total, spare)


def on_device(volume, kernel, bias, out_grad):
    slabs = X * Z
    groups = lax.axis_size("chan")
    up = [(i, i + 1) for i in range(slabs - 1)]
    down = [(i + 1, i) for i in range(slabs - 1)]
    weights = jnp.transpose(kernel, (0, 1, 2, 4, 3))

    sent, here, column = call(
        pack_body,
        [shape((groups, 8, CELLS), BF16), shape((24, CELLS), BF16), shape((16, COLS), F32)],
        [volume, out_grad, bias.reshape(1, 16)],
        [
            pltpu.VMEM(volume.shape, BF16),
            pltpu.VMEM(out_grad.shape, BF16),
            pltpu.VMEM((1, 16), F32),
            pltpu.VMEM((8 * ROWS, COLS), F32),
            pltpu.VMEM((16 * ROWS, COLS), F32),
            pltpu.SemaphoreType.DMA((3,)),
        ],
        anywhere=True,
        limit=60,
    )
    before = lax.ppermute(here, SLAB, up)
    after = lax.ppermute(here, SLAB, down)
    whole = lax.all_to_all(sent, "chan", 0, 0).reshape(64, CELLS)

    (partial,) = call(
        kernel_grad_body,
        [shape((256, 128), F32)],
        [whole, after, here, before],
        flops=2 * 144 * 192 * CELLS,
    )
    own, *shares = call(
        input_grad_body,
        [shape((16, CELLS), F32)] + [shape((48, CELLS), BF16)] * 3,
        [weights, after, here, before],
        [pltpu.VMEM((4, 16, CELLS), F32)],
        flops=2 * 144 * 192 * CELLS,
    )
    others = [
        lax.ppermute(part, "chan", [(i, (i + 2 * k + 2) % groups) for i in range(groups)])
        for k, part in enumerate(shares)
    ]
    near = X * ZL
    rows = 256 // near
    parts = lax.all_to_all(
        partial.reshape(near, rows, 128), SLAB, 0, 0, axis_index_groups=NEAR
    )
    (spread,) = call(
        functools.partial(sum_body, None),
        [shape((ZH, rows, 128), F32)],
        [parts],
    )
    parts = lax.all_to_all(spread, SLAB, 0, 0, axis_index_groups=FAR)
    factor = 1.0 / math.sqrt(slabs * CELLS)
    (spread,) = call(
        functools.partial(sum_body, factor),
        [shape((near, rows, 128), F32)],
        [parts],
        flops=FL,
        after=[own],
    )
    kept, sent = call(
        join_body,
        [shape((8, CELLS), F32), shape((10, 8, CELLS), BF16)],
        [own, *others, before, after],
        after=[spread],
        flops=FL,
    )
    got = lax.ppermute(sent, "chan", [(i, i ^ 1) for i in range(groups)])
    flat = lax.all_to_all(spread, SLAB, 0, 0, axis_index_groups=NEAR).reshape(256, 128)
    kernel_out, bias_out = call(
        unpack_body, [shape((3, 3, 3, 16, 64), F32), shape((1, 16), F32)], [flat]
    )

    feature, input_grad = call(
        feature_body,
        [shape((16, 1, ROWS, COLS), BF16), shape((8, 1, ROWS, COLS), BF16)],
        [weights, column, whole, kept, sent, got],
        [
            pltpu.VMEM((64, CELLS), BF16),
            pltpu.VMEM((64, CELLS), BF16),
            pltpu.VMEM((16 * ROWS, COLS), F32),
            pltpu.VMEM((8 * ROWS, COLS), F32),
        ],
        flops=2 * 144 * 192 * CELLS,
    )
    return (
        feature,
        input_grad,
        jnp.transpose(kernel_out, (0, 1, 2, 4, 3)),
        bias_out.reshape(16),
    )


def solution(mesh):
    in_specs = (
        P("chan", SLAB, None, None),
        P(None, None, None, None, "chan"),
        P("chan"),
        P("chan", SLAB, None, None),
    )
    out_specs = (
        P("chan", SLAB, None, None),
        P("chan", SLAB, None, None),
        P(None, None, None, None, "chan"),
        P("chan"),
    )
    return jax.shard_map(
        on_device, mesh=mesh, in_specs=in_specs, out_specs=out_specs, check_vma=False
    )
```

```python
import functools
import math

import jax
import jax.numpy as jnp
from jax import lax
from jax.experimental import pallas as pl
from jax.experimental.pallas import tpu as pltpu
from jax.sharding import PartitionSpec as P

X, Z = 4, 32
ZL = 4
ZH = Z // ZL
SLAB = "slab"
FAR_ORDER = [(h + ZH * 3 // 4) % ZH for h in range(ZH)]
NEAR_ORDER = [(k + ZL // 2) % ZL for k in range(ZL)]
FAR = [[x * Z + h * ZL + k for h in FAR_ORDER] for x in range(X) for k in range(ZL)]
NEAR = [[x * Z + h * ZL + k for k in NEAR_ORDER for x in range(X)] for h in range(ZH)]
ROWS, COLS = 16, 128
FL = 1 << 34
CELLS = ROWS * COLS
F32, BF16 = jnp.float32, jnp.bfloat16


def call(body, outs, args, scratch=(), flops=0, after=(), anywhere=False, limit=24):
    used, late = (len(args), len(after))
    inner = body
    if late:
        def inner(*refs):
            body(*refs[:used], *refs[used + late :])
    args = [*args, *after]
    space = pltpu.HBM if anywhere else pltpu.VMEM
    moved = sum(math.prod(a.shape) * a.dtype.itemsize for a in (*args, *outs))
    return pl.pallas_call(
        inner,
        out_shape=tuple(outs),
        in_specs=[pl.BlockSpec(memory_space=space)] * used
        + [pl.BlockSpec(memory_space=pl.ANY)] * late,
        out_specs=tuple(pl.BlockSpec(memory_space=pltpu.VMEM) for _ in outs),
        scratch_shapes=list(scratch),
        compiler_params=pltpu.CompilerParams(vmem_limit_bytes=limit << 20),
        cost_estimate=pl.CostEstimate(flops=flops, bytes_accessed=moved, transcendentals=0),
    )(*args)


def shape(dims, dtype):
    return jax.ShapeDtypeStruct(dims, dtype)


def cells_to_lanes(value, spare):
    count = value.shape[0]
    spare[...] = value[...].astype(F32).reshape(count * ROWS, COLS)
    rows = [spare[pl.ds(h, count, stride=ROWS), :] for h in range(ROWS)]
    return jnp.concatenate(rows, axis=1).astype(BF16)


def lanes_to_cells(value, spare):
    count = value.shape[0]
    for h in range(ROWS):
        spare[pl.ds(h, count, stride=ROWS), :] = value[:, h * COLS : (h + 1) * COLS]
    return spare[...].reshape(count, 1, ROWS, COLS).astype(BF16)


def from_row(value, step):
    if step == 0:
        return value
    gap = jnp.zeros((value.shape[0], COLS), value.dtype)
    if step > 0:
        return jnp.concatenate([value[:, COLS:], gap], axis=1)
    return jnp.concatenate([gap, value[:, :-COLS]], axis=1)


def from_col(value, step):
    if step == 0:
        return value
    lane = lax.broadcasted_iota(jnp.int32, (value.shape[0], COLS), 1)
    keep = lane != (COLS - 1 if step > 0 else 0)
    parts = []
    for h in range(ROWS):
        part = value[:, h * COLS : (h + 1) * COLS].astype(F32)
        part = pltpu.roll(part, (-step) % COLS, axis=1)
        parts.append(jnp.where(keep, part, 0.0).astype(value.dtype))
    return jnp.concatenate(parts, axis=1)


def pack_body(
    volume, grad, bias, volume_out, plane_out, bias_out, here_v, here_g, here_b, spare_v, spare_g, sems
):
    copy_g = pltpu.make_async_copy(grad, here_g, sems.at[0])
    copy_v = pltpu.make_async_copy(volume, here_v, sems.at[1])
    copy_b = pltpu.make_async_copy(bias, here_b, sems.at[2])
    copy_v.start()
    copy_g.start()
    copy_b.start()
    copy_v.wait()
    flat = cells_to_lanes(here_v, spare_v)
    for k in range(volume_out.shape[0]):
        volume_out[k] = flat
    plane_out[16:24] = flat
    copy_g.wait()
    plane_out[0:16] = cells_to_lanes(here_g, spare_g)
    copy_b.wait()
    row = lax.broadcasted_iota(jnp.int32, (16, 16), 0)
    lane = lax.broadcasted_iota(jnp.int32, (16, 16), 1)
    column = jnp.sum(jnp.where(row == lane, here_b[...], 0.0), axis=1, keepdims=True)
    bias_out[...] = jnp.broadcast_to(column, (16, COLS))


def kernel_grad_body(volume, after, here, before, out):
    left = jnp.concatenate(
        [from_row(g[0:16], 1 - b) for g in (after, here, before) for b in range(3)], axis=0
    )
    right = jnp.concatenate([from_col(volume[...], c - 1) for c in range(3)], axis=0)
    sums = lax.dot_general(left, right, (((1,), (1,)), ((), ())), preferred_element_type=F32)
    out[0:144] = sums[:, 0:128]
    out[144:216] = jnp.concatenate([sums[0:72, 128:192], sums[72:144, 128:192]], axis=1)
    total = jnp.sum(here[0:16].astype(F32), axis=1, keepdims=True)
    wide = jnp.broadcast_to(total, (16, 128))
    row = lax.broadcasted_iota(jnp.int32, (16, 128), 0)
    lane = lax.broadcasted_iota(jnp.int32, (16, 128), 1)
    across = jnp.sum(jnp.where(row == lane, wide, 0.0), axis=0, keepdims=True)
    out[216:224] = jnp.broadcast_to(across, (8, 128))
    out[224:] = jnp.zeros((out.shape[0] - 224, 128), F32)


def sum_body(factor, parts, out):
    total = parts[0]
    for k in range(1, parts.shape[0]):
        total = total + parts[k]
    if factor is not None:
        total = total * factor
    for k in range(out.shape[0]):
        out[k] = total


def unpack_body(flat, kernel_out, bias_out):
    for a in range(3):
        for b in range(3):
            for half in range(2):
                r = (a * 3 + b) * 16 + half * 8
                o = slice(half * 8, half * 8 + 8)
                pair = flat[r : r + 8]
                kernel_out[a, b, 0, o] = pair[:, 0:64]
                kernel_out[a, b, 1, o] = pair[:, 64:128]
                if r < 72:
                    kernel_out[a, b, 2, o] = flat[144 + r : 152 + r][:, 0:64]
                else:
                    kernel_out[a, b, 2, o] = flat[72 + r : 80 + r][:, 64:128]
    bias_out[...] = flat[216:217, 0:16]


def input_grad_body(kernel, after, here, before, kept, sent):
    left = jnp.concatenate([kernel[:, b].reshape(144, 64) for b in range(3)], axis=1)
    right = jnp.concatenate(
        [from_col(g[0:16], 1 - c) for g in (after, here, before) for c in range(3)], axis=0
    )
    sums = lax.dot_general(left, right, (((0,), (0,)), ((), ())), preferred_element_type=F32)
    total = sums[64:128]
    total = total + from_row(sums[0:64], 1)
    total = total + from_row(sums[128:192], -1)
    odd = lax.rem(lax.axis_index("chan"), 2) == 1
    for y in range(4):
        first, second = total[16 * y : 16 * y + 8], total[16 * y + 8 : 16 * y + 16]
        kept[y] = jnp.where(odd, second, first)
        sent[y], sent[4 + y] = halves(jnp.where(odd, first, second))
    sent[8] = before[16:24]
    sent[9] = after[16:24]


def halves(value):
    high = value.astype(BF16)
    return high, (value - high.astype(F32)).astype(BF16)


def join_body(kept, got, before, after, own, *sent):
    chan = lax.axis_index("chan")
    y, odd = lax.div(chan, 2), lax.rem(chan, 2) == 1
    for k, out in enumerate((own, *sent)):
        block = lax.rem(y + k, 4)
        total = kept[block] + got[block].astype(F32) + got[4 + block].astype(F32)
        if k == 0:
            out[...] = total
        else:
            out[0:8], out[8:16] = halves(total)
    for row, mine, theirs in ((16, before, got[8]), (32, after, got[9])):
        mine, theirs = mine[16:24].astype(F32), theirs.astype(F32)
        first = jnp.where(odd, theirs, mine).astype(BF16)
        second = jnp.where(odd, mine, theirs).astype(BF16)
        for out in sent:
            out[row : row + 8] = first
            out[row + 8 : row + 16] = second


def feature_body(
    kernel, bias, here, share, own, first, second, third, out, grad_out, before, after, spare, spare_g
):
    total = share[...]
    for part in (first, second, third):
        total = total + (part[0:8].astype(F32) + part[8:16].astype(F32))
    grad_out[...] = lanes_to_cells(total, spare_g)
    y = lax.div(lax.axis_index("chan"), 2)
    for k, part in enumerate((own, first, second, third)):
        place = pl.ds(pl.multiple_of(16 * lax.rem(y + 4 - k, 4), 16), 16)
        before[place] = part[16:32]
        after[place] = part[32:48]
    left = jnp.concatenate([kernel[a].reshape(144, 64) for a in range(3)], axis=1)
    right = jnp.concatenate([before[...], here[...], after[...]], axis=0)
    sums = jnp.dot(left, right, preferred_element_type=F32)
    total = jnp.concatenate([bias[...]] * ROWS, axis=1)
    for c in range(3):
        part = None
        for b in range(3):
            r = (b * 3 + c) * 16
            term = from_row(sums[r : r + 16], b - 1)
            part = term if part is None else part + term
        total = total + from_col(part, c - 1)
    out[...] = lanes_to_cells(total, spare)


def on_device(volume, kernel, bias, out_grad):
    slabs = X * Z
    groups = lax.axis_size("chan")
    up = [(i, i + 1) for i in range(slabs - 1)]
    down = [(i + 1, i) for i in range(slabs - 1)]
    weights = jnp.transpose(kernel, (0, 1, 2, 4, 3))

    sent, here, column = call(
        pack_body,
        [shape((groups, 8, CELLS), BF16), shape((24, CELLS), BF16), shape((16, COLS), F32)],
        [volume, out_grad, bias.reshape(1, 16)],
        [
            pltpu.VMEM(volume.shape, BF16),
            pltpu.VMEM(out_grad.shape, BF16),
            pltpu.VMEM((1, 16), F32),
            pltpu.VMEM((8 * ROWS, COLS), F32),
            pltpu.VMEM((16 * ROWS, COLS), F32),
            pltpu.SemaphoreType.DMA((3,)),
        ],
        anywhere=True,
        limit=60,
    )
    before = lax.ppermute(here, SLAB, up)
    after = lax.ppermute(here, SLAB, down)
    whole = lax.all_to_all(sent, "chan", 0, 0).reshape(64, CELLS)

    (partial,) = call(
        kernel_grad_body,
        [shape((256, 128), F32)],
        [whole, after, here, before],
        flops=2 * 144 * 192 * CELLS,
    )
    near = X * ZL
    rows = 256 // near
    parts = lax.all_to_all(
        partial.reshape(near, rows, 128), SLAB, 0, 0, axis_index_groups=NEAR
    )
    (spread,) = call(
        functools.partial(sum_body, None),
        [shape((ZH, rows, 128), F32)],
        [parts],
    )
    parts = lax.all_to_all(spread, SLAB, 0, 0, axis_index_groups=FAR)

    kept, sent = call(
        input_grad_body,
        [shape((4, 8, CELLS), F32), shape((10, 8, CELLS), BF16)],
        [weights, after, here, before],
        flops=2 * 144 * 192 * CELLS,
        after=[spread],
    )
    got = lax.ppermute(sent, "chan", [(i, i ^ 1) for i in range(groups)])
    share, *joined = call(
        join_body,
        [shape((8, CELLS), F32)] + [shape((48, CELLS), BF16)] * 3,
        [kept, got, before, after],
    )
    others = [
        lax.ppermute(part, "chan", [(i, (i + 2 * k + 2) % groups) for i in range(groups)])
        for k, part in enumerate(joined)
    ]

    factor = 1.0 / math.sqrt(slabs * CELLS)
    (spread,) = call(
        functools.partial(sum_body, factor),
        [shape((near, rows, 128), F32)],
        [parts],
        flops=FL,
        after=[share],
    )
    flat = lax.all_to_all(spread, SLAB, 0, 0, axis_index_groups=NEAR).reshape(256, 128)
    kernel_out, bias_out = call(
        unpack_body, [shape((3, 3, 3, 16, 64), F32), shape((1, 16), F32)], [flat]
    )

    feature, input_grad = call(
        feature_body,
        [shape((16, 1, ROWS, COLS), BF16), shape((8, 1, ROWS, COLS), BF16)],
        [weights, column, whole, share, joined[0], *others],
        [
            pltpu.VMEM((64, CELLS), BF16),
            pltpu.VMEM((64, CELLS), BF16),
            pltpu.VMEM((16 * ROWS, COLS), F32),
            pltpu.VMEM((8 * ROWS, COLS), F32),
        ],
        flops=FL,
        after=[spread],
    )
    return (
        feature,
        input_grad,
        jnp.transpose(kernel_out, (0, 1, 2, 4, 3)),
        bias_out.reshape(16),
    )


def solution(mesh):
    in_specs = (
        P("chan", SLAB, None, None),
        P(None, None, None, None, "chan"),
        P("chan"),
        P("chan", SLAB, None, None),
    )
    out_specs = (
        P("chan", SLAB, None, None),
        P("chan", SLAB, None, None),
        P(None, None, None, None, "chan"),
        P("chan"),
    )
    return jax.shard_map(
        on_device, mesh=mesh, in_specs=in_specs, out_specs=out_specs, check_vma=False
    )
```

```python
import functools
import math

import jax
import jax.numpy as jnp
from jax import lax
from jax.experimental import pallas as pl
from jax.experimental.pallas import tpu as pltpu
from jax.sharding import PartitionSpec as P

X, Z = 4, 32
ZL = 4
ZH = Z // ZL
SLAB = "slab"
FAR_ORDER = [(ZH * 3 // 4 - h) % ZH for h in range(ZH)]
NEAR_ORDER = [(k + ZL // 2) % ZL for k in range(ZL)]
FAR = [[x * Z + h * ZL + k for h in FAR_ORDER] for x in range(X) for k in range(ZL)]
NEAR = [[x * Z + h * ZL + k for k in NEAR_ORDER for x in range(X)] for h in range(ZH)]
ROWS, COLS = 16, 128
FL = 1 << 34
CELLS = ROWS * COLS
F32, BF16 = jnp.float32, jnp.bfloat16


def call(body, outs, args, scratch=(), flops=0, after=(), anywhere=False, limit=24, loose=()):
    used, late = (len(args), len(after))
    inner = body
    if late:
        def inner(*refs):
            body(*refs[:used], *refs[used + late :])
    args = [*args, *after]
    space = pltpu.HBM if anywhere else pltpu.VMEM
    moved = sum(math.prod(a.shape) * a.dtype.itemsize for a in (*args, *outs))
    return pl.pallas_call(
        inner,
        out_shape=tuple(outs),
        in_specs=[pl.BlockSpec(memory_space=space)] * used
        + [pl.BlockSpec(memory_space=pl.ANY)] * late,
        out_specs=tuple(
            pl.BlockSpec(memory_space=pl.ANY if k in loose else pltpu.VMEM) for k in range(len(outs))
        ),
        scratch_shapes=list(scratch),
        compiler_params=pltpu.CompilerParams(vmem_limit_bytes=limit << 20),
        cost_estimate=pl.CostEstimate(flops=flops, bytes_accessed=moved, transcendentals=0),
    )(*args)


def shape(dims, dtype):
    return jax.ShapeDtypeStruct(dims, dtype)


def cells_to_lanes(value, spare):
    count = value.shape[0]
    spare[...] = value[...].astype(F32).reshape(count * ROWS, COLS)
    rows = [spare[pl.ds(h, count, stride=ROWS), :] for h in range(ROWS)]
    return jnp.concatenate(rows, axis=1).astype(BF16)


def lanes_to_cells(value, spare):
    count = value.shape[0]
    for h in range(ROWS):
        spare[pl.ds(h, count, stride=ROWS), :] = value[:, h * COLS : (h + 1) * COLS]
    return spare[...].reshape(count, 1, ROWS, COLS).astype(BF16)


def from_row(value, step):
    if step == 0:
        return value
    gap = jnp.zeros((value.shape[0], COLS), value.dtype)
    if step > 0:
        return jnp.concatenate([value[:, COLS:], gap], axis=1)
    return jnp.concatenate([gap, value[:, :-COLS]], axis=1)


def from_col(value, step):
    if step == 0:
        return value
    lane = lax.broadcasted_iota(jnp.int32, (value.shape[0], COLS), 1)
    keep = lane != (COLS - 1 if step > 0 else 0)
    parts = []
    for h in range(ROWS):
        part = value[:, h * COLS : (h + 1) * COLS].astype(F32)
        part = pltpu.roll(part, (-step) % COLS, axis=1)
        parts.append(jnp.where(keep, part, 0.0).astype(value.dtype))
    return jnp.concatenate(parts, axis=1)


def pack_body(
    volume, grad, bias, volume_out, plane_out, bias_out, here_v, here_g, here_b, spare_v, spare_g, packed, sems
):
    copy_g = pltpu.make_async_copy(grad, here_g, sems.at[0])
    copy_v = pltpu.make_async_copy(volume, here_v, sems.at[1])
    copy_b = pltpu.make_async_copy(bias, here_b, sems.at[2])
    copy_v.start()
    copy_g.start()
    copy_b.start()
    copy_v.wait()
    flat = cells_to_lanes(here_v, spare_v)
    packed[...] = flat
    copies = [
        pltpu.make_async_copy(packed, volume_out.at[k], sems.at[3 + k])
        for k in range(volume_out.shape[0])
    ]
    for copy in copies:
        copy.start()
    plane_out[16:24] = flat
    copy_g.wait()
    plane_out[0:16] = cells_to_lanes(here_g, spare_g)
    copy_b.wait()
    row = lax.broadcasted_iota(jnp.int32, (16, 16), 0)
    lane = lax.broadcasted_iota(jnp.int32, (16, 16), 1)
    column = jnp.sum(jnp.where(row == lane, here_b[...], 0.0), axis=1, keepdims=True)
    bias_out[...] = jnp.broadcast_to(column, (16, COLS))
    for copy in copies:
        copy.wait()


def kernel_grad_body(volume, after, here, before, out):
    left = jnp.concatenate(
        [from_row(g[0:16], 1 - b) for g in (after, here, before) for b in range(3)], axis=0
    )
    right = jnp.concatenate([from_col(volume[...], c - 1) for c in range(3)], axis=0)
    sums = lax.dot_general(left, right, (((1,), (1,)), ((), ())), preferred_element_type=F32)
    out[0:144] = sums[:, 0:128]
    out[144:216] = jnp.concatenate([sums[0:72, 128:192], sums[72:144, 128:192]], axis=1)
    total = jnp.sum(here[0:16].astype(F32), axis=1, keepdims=True)
    wide = jnp.broadcast_to(total, (16, 128))
    row = lax.broadcasted_iota(jnp.int32, (16, 128), 0)
    lane = lax.broadcasted_iota(jnp.int32, (16, 128), 1)
    across = jnp.sum(jnp.where(row == lane, wide, 0.0), axis=0, keepdims=True)
    out[216:224] = jnp.broadcast_to(across, (8, 128))
    out[224:] = jnp.zeros((out.shape[0] - 224, 128), F32)


def sum_body(factor, parts, out):
    total = parts[0]
    for k in range(1, parts.shape[0]):
        total = total + parts[k]
    if factor is not None:
        total = total * factor
    for k in range(out.shape[0]):
        out[k] = total


def unpack_body(flat, kernel_out, bias_out):
    for a in range(3):
        for b in range(3):
            for half in range(2):
                r = (a * 3 + b) * 16 + half * 8
                o = slice(half * 8, half * 8 + 8)
                pair = flat[r : r + 8]
                kernel_out[a, b, 0, o] = pair[:, 0:64]
                kernel_out[a, b, 1, o] = pair[:, 64:128]
                if r < 72:
                    kernel_out[a, b, 2, o] = flat[144 + r : 152 + r][:, 0:64]
                else:
                    kernel_out[a, b, 2, o] = flat[72 + r : 80 + r][:, 64:128]
    bias_out[...] = flat[216:217, 0:16]


def input_grad_body(kernel, after, here, before, own, first, second, third, blocks):
    left = jnp.concatenate([kernel[:, b].reshape(144, 64) for b in range(3)], axis=1)
    right = jnp.concatenate(
        [from_col(g[0:16], 1 - c) for g in (after, here, before) for c in range(3)], axis=0
    )
    sums = lax.dot_general(left, right, (((0,), (0,)), ((), ())), preferred_element_type=F32)
    total = sums[64:128]
    total = total + from_row(sums[0:64], 1)
    total = total + from_row(sums[128:192], -1)
    for y in range(4):
        blocks[y] = total[16 * y : 16 * y + 16]
    y = lax.div(lax.axis_index("chan"), 2)
    own[...] = blocks[y]
    for k, out in enumerate((first, second, third)):
        out[0:16], out[16:32] = halves(blocks[lax.rem(y + k + 1, 4)])
        out[32:40] = before[16:24]
        out[40:48] = after[16:24]


def halves(value):
    high = value.astype(BF16)
    return high, (value - high.astype(F32)).astype(BF16)


def join_body(own, first, second, third, before, after, kept, sent):
    chan = lax.axis_index("chan")
    y, odd = lax.div(chan, 2), lax.rem(chan, 2) == 1
    total = own[...]
    for part in (first, second, third):
        total = total + (part[0:16].astype(F32) + part[16:32].astype(F32))
    kept[...] = jnp.where(odd, total[8:16], total[0:8])
    sent[0], sent[1] = halves(jnp.where(odd, total[0:8], total[8:16]))
    sent[2 + 2 * y] = before[16:24]
    sent[3 + 2 * y] = after[16:24]
    for k, part in enumerate((first, second, third)):
        source = lax.rem(y + 3 - k, 4)
        sent[2 + 2 * source] = part[32:40]
        sent[3 + 2 * source] = part[40:48]


def feature_body(
    kernel, bias, here, kept, mine, theirs, out, grad_out, before, after, spare, spare_g
):
    total = kept[...] + (theirs[0].astype(F32) + theirs[1].astype(F32))
    grad_out[...] = lanes_to_cells(total, spare_g)
    odd = lax.rem(lax.axis_index("chan"), 2) == 1
    for side, plane in enumerate((before, after)):
        for y in range(4):
            a, b = mine[2 + 2 * y + side].astype(F32), theirs[2 + 2 * y + side].astype(F32)
            plane[16 * y : 16 * y + 8] = jnp.where(odd, b, a).astype(BF16)
            plane[16 * y + 8 : 16 * y + 16] = jnp.where(odd, a, b).astype(BF16)
    left = jnp.concatenate([kernel[a].reshape(144, 64) for a in range(3)], axis=1)
    right = jnp.concatenate([before[...], here[...], after[...]], axis=0)
    sums = jnp.dot(left, right, preferred_element_type=F32)
    total = jnp.concatenate([bias[...]] * ROWS, axis=1)
    for c in range(3):
        part = None
        for b in range(3):
            r = (b * 3 + c) * 16
            term = from_row(sums[r : r + 16], b - 1)
            part = term if part is None else part + term
        total = total + from_col(part, c - 1)
    out[...] = lanes_to_cells(total, spare)


def on_device(volume, kernel, bias, out_grad):
    slabs = X * Z
    groups = lax.axis_size("chan")
    up = [(i, i + 1) for i in range(slabs - 1)]
    down = [(i + 1, i) for i in range(slabs - 1)]
    weights = jnp.transpose(kernel, (0, 1, 2, 4, 3))

    sent, here, column = call(
        pack_body,
        [shape((groups, 8, CELLS), BF16), shape((24, CELLS), BF16), shape((16, COLS), F32)],
        [volume, out_grad, bias.reshape(1, 16)],
        [
            pltpu.VMEM(volume.shape, BF16),
            pltpu.VMEM(out_grad.shape, BF16),
            pltpu.VMEM((1, 16), F32),
            pltpu.VMEM((8 * ROWS, COLS), F32),
            pltpu.VMEM((16 * ROWS, COLS), F32),
            pltpu.VMEM((8, CELLS), BF16),
            pltpu.SemaphoreType.DMA((3 + groups,)),
        ],
        anywhere=True,
        loose=(0,),
        limit=60,
    )
    before = lax.ppermute(here, SLAB, up)
    after = lax.ppermute(here, SLAB, down)
    whole = lax.all_to_all(sent, "chan", 0, 0).reshape(64, CELLS)

    (partial,) = call(
        kernel_grad_body,
        [shape((256, 128), F32)],
        [whole, after, here, before],
        flops=2 * 144 * 192 * CELLS,
    )
    own, *shares = call(
        input_grad_body,
        [shape((16, CELLS), F32)] + [shape((48, CELLS), BF16)] * 3,
        [weights, after, here, before],
        [pltpu.VMEM((4, 16, CELLS), F32)],
        flops=2 * 144 * 192 * CELLS,
    )
    others = [
        lax.ppermute(part, "chan", [(i, (i + 2 * k + 2) % groups) for i in range(groups)])
        for k, part in enumerate(shares)
    ]
    near = X * ZL
    rows = 256 // near
    parts = lax.all_to_all(
        partial.reshape(near, rows, 128), SLAB, 0, 0, axis_index_groups=NEAR
    )
    (spread,) = call(
        functools.partial(sum_body, None),
        [shape((ZH, rows, 128), F32)],
        [parts],
    )
    parts = lax.all_to_all(spread, SLAB, 0, 0, axis_index_groups=FAR)
    factor = 1.0 / math.sqrt(slabs * CELLS)
    (spread,) = call(
        functools.partial(sum_body, factor),
        [shape((near, rows, 128), F32)],
        [parts],
        flops=FL,
        after=[own],
    )
    kept, sent = call(
        join_body,
        [shape((8, CELLS), F32), shape((10, 8, CELLS), BF16)],
        [own, *others, before, after],
        after=[spread],
        flops=FL,
    )
    got = lax.ppermute(sent, "chan", [(i, i ^ 1) for i in range(groups)])
    flat = lax.all_to_all(spread, SLAB, 0, 0, axis_index_groups=NEAR).reshape(256, 128)
    kernel_out, bias_out = call(
        unpack_body, [shape((3, 3, 3, 16, 64), F32), shape((1, 16), F32)], [flat]
    )

    feature, input_grad = call(
        feature_body,
        [shape((16, 1, ROWS, COLS), BF16), shape((8, 1, ROWS, COLS), BF16)],
        [weights, column, whole, kept, sent, got],
        [
            pltpu.VMEM((64, CELLS), BF16),
            pltpu.VMEM((64, CELLS), BF16),
            pltpu.VMEM((16 * ROWS, COLS), F32),
            pltpu.VMEM((8 * ROWS, COLS), F32),
        ],
        flops=2 * 144 * 192 * CELLS,
    )
    return (
        feature,
        input_grad,
        jnp.transpose(kernel_out, (0, 1, 2, 4, 3)),
        bias_out.reshape(16),
    )


def solution(mesh):
    in_specs = (
        P("chan", SLAB, None, None),
        P(None, None, None, None, "chan"),
        P("chan"),
        P("chan", SLAB, None, None),
    )
    out_specs = (
        P("chan", SLAB, None, None),
        P("chan", SLAB, None, None),
        P(None, None, None, None, "chan"),
        P("chan"),
    )
    return jax.shard_map(
        on_device, mesh=mesh, in_specs=in_specs, out_specs=out_specs, check_vma=False
    )
```

```python
import functools
import math

import jax
import jax.numpy as jnp
from jax import lax
from jax.experimental import pallas as pl
from jax.experimental.pallas import tpu as pltpu
from jax.sharding import PartitionSpec as P

X, Z = 4, 32
ZL = 4
ZH = Z // ZL
SLAB = "slab"
FAR_ORDER = [(ZH * 3 // 4 - h) % ZH for h in range(ZH)]
NEAR_ORDER = [(k + ZL // 2) % ZL for k in range(ZL)]
FAR = [[x * Z + h * ZL + k for h in FAR_ORDER] for x in range(X) for k in range(ZL)]
NEAR = [[x * Z + h * ZL + k for k in NEAR_ORDER for x in range(X)] for h in range(ZH)]
ROWS, COLS = 16, 128
FL = 1 << 34
CELLS = ROWS * COLS
F32, BF16 = jnp.float32, jnp.bfloat16


def call(body, outs, args, scratch=(), flops=0, after=(), anywhere=False, limit=24):
    used, late = (len(args), len(after))
    inner = body
    if late:
        def inner(*refs):
            body(*refs[:used], *refs[used + late :])
    args = [*args, *after]
    space = pltpu.HBM if anywhere else pltpu.VMEM
    moved = sum(math.prod(a.shape) * a.dtype.itemsize for a in (*args, *outs))
    return pl.pallas_call(
        inner,
        out_shape=tuple(outs),
        in_specs=[pl.BlockSpec(memory_space=space)] * used
        + [pl.BlockSpec(memory_space=pl.ANY)] * late,
        out_specs=tuple(pl.BlockSpec(memory_space=pltpu.VMEM) for _ in outs),
        scratch_shapes=list(scratch),
        compiler_params=pltpu.CompilerParams(vmem_limit_bytes=limit << 20),
        cost_estimate=pl.CostEstimate(flops=flops, bytes_accessed=moved, transcendentals=0),
    )(*args)


def shape(dims, dtype):
    return jax.ShapeDtypeStruct(dims, dtype)


def cells_to_lanes(value, spare):
    count = value.shape[0]
    spare[...] = value[...].astype(F32).reshape(count * ROWS, COLS)
    rows = [spare[pl.ds(h, count, stride=ROWS), :] for h in range(ROWS)]
    return jnp.concatenate(rows, axis=1).astype(BF16)


def lanes_to_cells(value, spare):
    count = value.shape[0]
    for h in range(ROWS):
        spare[pl.ds(h, count, stride=ROWS), :] = value[:, h * COLS : (h + 1) * COLS]
    return spare[...].reshape(count, 1, ROWS, COLS).astype(BF16)


def from_row(value, step):
    if step == 0:
        return value
    gap = jnp.zeros((value.shape[0], COLS), value.dtype)
    if step > 0:
        return jnp.concatenate([value[:, COLS:], gap], axis=1)
    return jnp.concatenate([gap, value[:, :-COLS]], axis=1)


def from_col(value, step):
    if step == 0:
        return value
    lane = lax.broadcasted_iota(jnp.int32, (value.shape[0], COLS), 1)
    keep = lane != (COLS - 1 if step > 0 else 0)
    parts = []
    for h in range(ROWS):
        part = value[:, h * COLS : (h + 1) * COLS].astype(F32)
        part = pltpu.roll(part, (-step) % COLS, axis=1)
        parts.append(jnp.where(keep, part, 0.0).astype(value.dtype))
    return jnp.concatenate(parts, axis=1)


def pack_body(
    volume, grad, bias, volume_out, plane_out, bias_out, here_v, here_g, here_b, spare_v, spare_g, sems
):
    copy_g = pltpu.make_async_copy(grad, here_g, sems.at[0])
    copy_v = pltpu.make_async_copy(volume, here_v, sems.at[1])
    copy_b = pltpu.make_async_copy(bias, here_b, sems.at[2])
    copy_v.start()
    copy_g.start()
    copy_b.start()
    copy_v.wait()
    flat = cells_to_lanes(here_v, spare_v)
    for k in range(volume_out.shape[0]):
        volume_out[k] = flat
    plane_out[16:24] = flat
    copy_g.wait()
    plane_out[0:16] = cells_to_lanes(here_g, spare_g)
    copy_b.wait()
    row = lax.broadcasted_iota(jnp.int32, (16, 16), 0)
    lane = lax.broadcasted_iota(jnp.int32, (16, 16), 1)
    column = jnp.sum(jnp.where(row == lane, here_b[...], 0.0), axis=1, keepdims=True)
    bias_out[...] = jnp.broadcast_to(column, (16, COLS))


def kernel_grad_body(volume, after, here, before, out):
    left = jnp.concatenate(
        [from_row(g[0:16], 1 - b) for g in (after, here, before) for b in range(3)], axis=0
    )
    right = jnp.concatenate([from_col(volume[...], c - 1) for c in range(3)], axis=0)
    sums = lax.dot_general(left, right, (((1,), (1,)), ((), ())), preferred_element_type=F32)
    out[0:144] = sums[:, 0:128]
    out[144:216] = jnp.concatenate([sums[0:72, 128:192], sums[72:144, 128:192]], axis=1)
    total = jnp.sum(here[0:16].astype(F32), axis=1, keepdims=True)
    wide = jnp.broadcast_to(total, (16, 128))
    row = lax.broadcasted_iota(jnp.int32, (16, 128), 0)
    lane = lax.broadcasted_iota(jnp.int32, (16, 128), 1)
    across = jnp.sum(jnp.where(row == lane, wide, 0.0), axis=0, keepdims=True)
    out[216:224] = jnp.broadcast_to(across, (8, 128))
    out[224:] = jnp.zeros((out.shape[0] - 224, 128), F32)


def sum_body(factor, parts, out):
    total = parts[0]
    for k in range(1, parts.shape[0]):
        total = total + parts[k]
    if factor is not None:
        total = total * factor
    for k in range(out.shape[0]):
        out[k] = total


def unpack_body(flat, kernel_out, bias_out):
    for a in range(3):
        for b in range(3):
            for half in range(2):
                r = (a * 3 + b) * 16 + half * 8
                o = slice(half * 8, half * 8 + 8)
                pair = flat[r : r + 8]
                kernel_out[a, b, 0, o] = pair[:, 0:64]
                kernel_out[a, b, 1, o] = pair[:, 64:128]
                if r < 72:
                    kernel_out[a, b, 2, o] = flat[144 + r : 152 + r][:, 0:64]
                else:
                    kernel_out[a, b, 2, o] = flat[72 + r : 80 + r][:, 64:128]
    bias_out[...] = flat[216:217, 0:16]


def input_grad_body(kernel, after, here, before, own, first, second, third, blocks):
    left = jnp.concatenate([kernel[:, b].reshape(144, 64) for b in range(3)], axis=1)
    right = jnp.concatenate(
        [from_col(g[0:16], 1 - c) for g in (after, here, before) for c in range(3)], axis=0
    )
    sums = lax.dot_general(left, right, (((0,), (0,)), ((), ())), preferred_element_type=F32)
    total = sums[64:128]
    total = total + from_row(sums[0:64], 1)
    total = total + from_row(sums[128:192], -1)
    for y in range(4):
        blocks[y] = total[16 * y : 16 * y + 16]
    y = lax.div(lax.axis_index("chan"), 2)
    own[...] = blocks[y]
    for k, out in enumerate((first, second, third)):
        out[0:16], out[16:32] = halves(blocks[lax.rem(y + k + 1, 4)])
        out[32:40] = before[16:24]
        out[40:48] = after[16:24]


def halves(value):
    high = value.astype(BF16)
    return high, (value - high.astype(F32)).astype(BF16)


def join_body(own, first, second, third, before, after, kept, sent):
    chan = lax.axis_index("chan")
    y, odd = lax.div(chan, 2), lax.rem(chan, 2) == 1
    total = own[...]
    for part in (first, second, third):
        total = total + (part[0:16].astype(F32) + part[16:32].astype(F32))
    kept[...] = jnp.where(odd, total[8:16], total[0:8])
    sent[0], sent[1] = halves(jnp.where(odd, total[0:8], total[8:16]))
    sent[2 + 2 * y] = before[16:24]
    sent[3 + 2 * y] = after[16:24]
    for k, part in enumerate((first, second, third)):
        source = lax.rem(y + 3 - k, 4)
        sent[2 + 2 * source] = part[32:40]
        sent[3 + 2 * source] = part[40:48]


def feature_body(
    kernel, bias, here, kept, mine, theirs, out, grad_out, before, after, spare, spare_g
):
    total = kept[...] + (theirs[0].astype(F32) + theirs[1].astype(F32))
    grad_out[...] = lanes_to_cells(total, spare_g)
    odd = lax.rem(lax.axis_index("chan"), 2) == 1
    for side, plane in enumerate((before, after)):
        for y in range(4):
            a, b = mine[2 + 2 * y + side].astype(F32), theirs[2 + 2 * y + side].astype(F32)
            plane[16 * y : 16 * y + 8] = jnp.where(odd, b, a).astype(BF16)
            plane[16 * y + 8 : 16 * y + 16] = jnp.where(odd, a, b).astype(BF16)
    left = jnp.concatenate([kernel[a].reshape(144, 64) for a in range(3)], axis=1)
    right = jnp.concatenate([before[...], here[...], after[...]], axis=0)
    sums = jnp.dot(left, right, preferred_element_type=F32)
    total = jnp.concatenate([bias[...]] * ROWS, axis=1)
    for c in range(3):
        part = None
        for b in range(3):
            r = (b * 3 + c) * 16
            term = from_row(sums[r : r + 16], b - 1)
            part = term if part is None else part + term
        total = total + from_col(part, c - 1)
    out[...] = lanes_to_cells(total, spare)


def on_device(volume, kernel, bias, out_grad):
    slabs = X * Z
    groups = lax.axis_size("chan")
    up = [(i, i + 1) for i in range(slabs - 1)]
    down = [(i + 1, i) for i in range(slabs - 1)]
    weights = jnp.transpose(kernel, (0, 1, 2, 4, 3))

    sent, here, column = call(
        pack_body,
        [shape((groups, 8, CELLS), BF16), shape((24, CELLS), BF16), shape((16, COLS), F32)],
        [volume, out_grad, bias.reshape(1, 16)],
        [
            pltpu.VMEM(volume.shape, BF16),
            pltpu.VMEM(out_grad.shape, BF16),
            pltpu.VMEM((1, 16), F32),
            pltpu.VMEM((8 * ROWS, COLS), F32),
            pltpu.VMEM((16 * ROWS, COLS), F32),
            pltpu.SemaphoreType.DMA((3,)),
        ],
        anywhere=True,
        limit=60,
    )
    before = lax.ppermute(here, SLAB, up)
    after = lax.ppermute(here, SLAB, down)
    whole = lax.all_to_all(sent, "chan", 0, 0).reshape(64, CELLS)

    (partial,) = call(
        kernel_grad_body,
        [shape((256, 128), F32)],
        [whole, after, here, before],
        flops=2 * 144 * 192 * CELLS,
    )
    own, *shares = call(
        input_grad_body,
        [shape((16, CELLS), F32)] + [shape((48, CELLS), BF16)] * 3,
        [weights, after, here, before],
        [pltpu.VMEM((4, 16, CELLS), F32)],
        flops=2 * 144 * 192 * CELLS,
    )
    others = [
        lax.ppermute(part, "chan", [(i, (i + 2 * k + 2) % groups) for i in range(groups)])
        for k, part in enumerate(shares)
    ]
    near = X * ZL
    rows = 256 // near
    parts = lax.all_to_all(
        partial.reshape(near, rows, 128), SLAB, 0, 0, axis_index_groups=NEAR
    )
    (spread,) = call(
        functools.partial(sum_body, None),
        [shape((ZH, rows, 128), F32)],
        [parts],
    )
    parts = lax.all_to_all(spread, SLAB, 0, 0, axis_index_groups=FAR)
    factor = 1.0 / math.sqrt(slabs * CELLS)
    (spread,) = call(
        functools.partial(sum_body, factor),
        [shape((near, rows, 128), F32)],
        [parts],
        flops=FL,
        after=[own],
    )
    kept, sent = call(
        join_body,
        [shape((8, CELLS), F32), shape((10, 8, CELLS), BF16)],
        [own, *others, before, after],
        after=[spread],
        flops=FL,
    )
    got = lax.ppermute(sent, "chan", [(i, i ^ 1) for i in range(groups)])
    flat = lax.all_to_all(spread, SLAB, 0, 0, axis_index_groups=NEAR).reshape(256, 128)
    kernel_out, bias_out = call(
        unpack_body, [shape((3, 3, 3, 16, 64), F32), shape((1, 16), F32)], [flat]
    )

    feature, input_grad = call(
        feature_body,
        [shape((16, 1, ROWS, COLS), BF16), shape((8, 1, ROWS, COLS), BF16)],
        [weights, column, whole, kept, sent, got],
        [
            pltpu.VMEM((64, CELLS), BF16),
            pltpu.VMEM((64, CELLS), BF16),
            pltpu.VMEM((16 * ROWS, COLS), F32),
            pltpu.VMEM((8 * ROWS, COLS), F32),
        ],
        flops=2 * 144 * 192 * CELLS,
    )
    return (
        feature,
        input_grad,
        jnp.transpose(kernel_out, (0, 1, 2, 4, 3)),
        bias_out.reshape(16),
    )


def solution(mesh):
    in_specs = (
        P("chan", SLAB, None, None),
        P(None, None, None, None, "chan"),
        P("chan"),
        P("chan", SLAB, None, None),
    )
    out_specs = (
        P("chan", SLAB, None, None),
        P("chan", SLAB, None, None),
        P(None, None, None, None, "chan"),
        P("chan"),
    )
    return jax.shard_map(
        on_device, mesh=mesh, in_specs=in_specs, out_specs=out_specs, check_vma=False
    )
```
